32 devices in a mesh: seg: 4 (over x, core), space: 8 (over z, y).
Axes of the slice: x: 2, y: 2, z: 4, core: 2. Of those that a mesh axis runs over, the one named last changes fastest.
Arguments:
- directions: float32 [4, 16, 32, 64, 128], P('seg', None, 'space'), may hold values from -100 to 100
- adjoint: float32 [4, 32, 64, 128], P('seg', 'space'), may hold values from -1000 to 1000
- velocity: float32 [4, 3, 32, 64, 128], P('seg', None, 'space'), may hold values from -1 to 1
- diffusivity: float32 [4, 32, 64, 128], P('seg', 'space'), may hold values from 0.05 to 0.15
- objective_source: float32 [4, 32, 64, 128], P('seg', 'space'), may hold values from -6 to 6
- segment_start: int32 [4], P('seg'), may hold values from 0 to 999
Outputs:
- basis_rows: float32 [4, 16, 32, 64, 128], P('seg', None, 'space')
- factor_upper: float32 [4, 16, 16], P('seg')
- coefficients: float32 [4, 16], P('seg')
- shadow: float32 [4, 32, 64, 128], P('seg', 'space')
- gradient: float32 [32, 64, 128], P('space', 'seg')
The draws below stay inside these ranges and needn't reach their ends.
All inputs are finite; a program needn't handle non-finite values.
Results may differ from the reference program's by a relative error of at most 0.0003.
Values sent between devices are 32-bit elements; how exact they have to be, the bound alone decides.
No kernel may reach another device: no remote copies, remote signals or barrier semaphores. Data moves between devices by JAX's collectives and lax.ppermute only.
A program may use at most 64 MiB of HBM per device.

```python
import math
import jax
import jax.numpy as jnp
from jax import lax

M = 16
NY = 64
NZ = 128
SEGS = 4
NX = 32


def common_fields(key):
    base = jax.random.fold_in(key, 11)
    noise = jnp.clip(jax.random.normal(jax.random.fold_in(base, 1), (SEGS, M, NX, NY, NZ), jnp.float32), -5.0, 5.0)
    shared = jnp.clip(jax.random.normal(jax.random.fold_in(base, 2), (SEGS, 1, NX, NY, NZ), jnp.float32), -5.0, 5.0)
    mixing = jax.random.uniform(jax.random.fold_in(base, 3), (SEGS, M, 1, 1, 1), jnp.float32, 0.5, 1.0)
    fields = noise + mixing * shared
    weights = jax.random.uniform(jax.random.fold_in(base, 5), (SEGS, M, 1, 1, 1), jnp.float32, -0.6, 0.6)
    lone = jnp.clip(jax.random.normal(jax.random.fold_in(base, 6), (SEGS, NX, NY, NZ), jnp.float32), -5.0, 5.0)
    adjoint_field = lone + jnp.sum(weights * fields, axis=1)
    return (fields, adjoint_field)


def draw_directions(key, part):
    return common_fields(key)[0]


def draw_adjoint(key, part):
    return common_fields(key)[1]


def plant(result, key, smallest, high):
    spot = [jax.random.randint(jax.random.fold_in(key, axis), (), 0, length) for axis, length in enumerate(result.shape)]
    widest = result.shape.index(max(result.shape))
    next_to = spot[:widest] + [(spot[widest] + 1) % result.shape[widest]] + spot[widest + 1:]
    return result.at[tuple(spot)].set(smallest).at[tuple(next_to)].set(high)


def shard_levels(stream_key, dims, split, low, largest):
    loudness, own = 1.0, jax.random.fold_in(stream_key, 6)
    for axis_at, blocks in split:
        heights = jnp.exp(jax.random.uniform(jax.random.fold_in(own, axis_at), (blocks,), jnp.float32, low / len(split), largest / len(split)))
        loudness = loudness * jnp.repeat(heights, dims[axis_at] // blocks).reshape([-1 if axis == axis_at else 1 for axis in range(len(dims))])
    return loudness


def centred(own_key, shape, deviation, most, cuts=(), kind=jnp.bfloat16):
    drawn = deviation * jax.random.normal(own_key, shape, jnp.float32)
    if cuts:
        drawn = drawn * shard_levels(own_key, shape, cuts, -0.22, 0.18)
    return jnp.clip(drawn, -most, most).astype(kind)


def setup_inputs(seed: int = 0) -> dict:
    seeds = jax.random.split(jax.random.key(seed), 7)
    return {
        "directions": draw_directions(jax.random.fold_in(seeds[6], 71), 0),
        "adjoint": draw_adjoint(jax.random.fold_in(seeds[6], 71), 0),
        "velocity": centred(seeds[2], (SEGS, 3, NX, NY, NZ), 0.3, 1.0, ((0, 4), (2, 8)), jnp.float32),
        "diffusivity": jnp.clip(0.05 + 0.10000001 * jax.random.uniform(seeds[3], (SEGS, NX, NY, NZ), jnp.float32) ** shard_levels(seeds[3], (SEGS, NX, NY, NZ), ((0, 4), (1, 8)), -0.2, 0.2), 0.05, 0.15),
        "objective_source": centred(seeds[4], (SEGS, NX, NY, NZ), 1.0, 6.0, ((0, 4), (1, 8)), jnp.float32),
        "segment_start": plant(jax.random.randint(seeds[5], (SEGS,), 0, 1000), jax.random.fold_in(seeds[5], 1), 0, 999).astype(jnp.int32),
    }


def modulation(window_start, section):
    phase_step = (window_start + 2 - section) % 64
    return 1.0 + 0.5 * jnp.sin(2.0 * math.pi * phase_step.astype(jnp.float32) / 64.0)

def advance(stacked, diffusivity, velocity, strength):
    forward_x = jnp.roll(stacked, -1, axis=1)
    behind_x = jnp.roll(stacked, 1, axis=1)
    wall_zero = jnp.zeros_like(stacked[:, :, :1])
    forward_y = jnp.concatenate([stacked[:, :, 1:], wall_zero], axis=2)
    behind_y = jnp.concatenate([wall_zero, stacked[:, :, :-1]], axis=2)
    forward_z = jnp.roll(stacked, -1, axis=3)
    behind_z = jnp.roll(stacked, 1, axis=3)
    laplace = forward_x + behind_x + forward_y + behind_y + forward_z + behind_z - 6.0 * stacked
    transport = velocity[0] * (forward_x - behind_x) + velocity[1] * (forward_y - behind_y) + velocity[2] * (forward_z - behind_z)
    return stacked + diffusivity * laplace + 0.5 * strength * transport

def one_segment(directions, adjoint, velocity, diffusivity, source, window_start):
    stacked = jnp.concatenate([directions, adjoint[None]], axis=0)
    stacked = advance(stacked, diffusivity, velocity, modulation(window_start, 1))
    stacked = stacked.at[-1].add(source)
    first_adjoint = stacked[-1]
    stacked = advance(stacked, diffusivity, velocity, modulation(window_start, 2))
    stacked = stacked.at[-1].add(source)
    flattened = stacked.reshape(M + 1, -1)
    cell_count = NX * NY * NZ
    summed = jnp.dot(flattened[:M], flattened.T, precision=lax.Precision.HIGHEST) / cell_count
    triangle = jnp.linalg.cholesky(summed[:, :M])
    inverse = jax.scipy.linalg.solve_triangular(triangle, jnp.eye(M, dtype=triangle.dtype), lower=True)
    basis_rows = jnp.dot(inverse, flattened[:M], precision=lax.Precision.HIGHEST)
    coefficients = jnp.dot(inverse, summed[:, M], precision=lax.Precision.HIGHEST)
    shadow = flattened[M] - jnp.dot(coefficients, basis_rows, precision=lax.Precision.HIGHEST)
    shadow = shadow.reshape(NX, NY, NZ)
    return (basis_rows.reshape(M, NX, NY, NZ), triangle.T, coefficients, shadow, first_adjoint + shadow)

def reference(directions, adjoint, velocity, diffusivity, objective_source, segment_start):
    basis_all = []
    factor_all = []
    coef_all = []
    shadow_all = []
    gradient = jnp.zeros((NX, NY, NZ), jnp.float32)
    for segment in range(SEGS):
        outputs = one_segment(directions[segment], adjoint[segment], velocity[segment], diffusivity[segment], objective_source[segment], segment_start[segment])
        basis_all.append(outputs[0])
        factor_all.append(outputs[1])
        coef_all.append(outputs[2])
        shadow_all.append(outputs[3])
        gradient = gradient + outputs[4]
    return (jnp.stack(basis_all), jnp.stack(factor_all), jnp.stack(coef_all), jnp.stack(shadow_all), gradient)
```

```python
import functools
import math

import jax
import jax.numpy as jnp
from jax import lax
from jax.experimental import pallas as pl
from jax.experimental.pallas import tpu as pltpu
from jax.sharding import PartitionSpec as P

SUB = 8
HIGH = lax.Precision.HIGHEST
VMEM_SPEC = pl.BlockSpec(memory_space=pltpu.VMEM)
SMEM_SPEC = pl.BlockSpec(memory_space=pltpu.SMEM)
ANY_SPEC = pl.BlockSpec(memory_space=pl.ANY)


def modulation(window_start, section):
    phase_step = (window_start + 2 - section) % 64
    return 1.0 + 0.5 * jnp.sin(2.0 * math.pi * phase_step.astype(jnp.float32) / 64.0)


def call(body, name, outs, specs, args, scratch=(), flops=0, moved=0):
    return pl.pallas_call(
        body,
        out_shape=outs,
        in_specs=specs,
        out_specs=jax.tree.map(lambda _: VMEM_SPEC, outs) if name != "pack" else [ANY_SPEC] * len(outs),
        scratch_shapes=scratch,
        name=name,
        cost_estimate=pl.CostEstimate(flops=flops, transcendentals=0, bytes_accessed=moved),
        compiler_params=pltpu.CompilerParams(vmem_limit_bytes=40 * 1024 * 1024),
    )(*args)


def layer_of(odd, position, layers):
    return position + odd * (layers - 1 - 2 * position)


def pack_kernel(count, layers, place, dirs, adj, first, second, sems):
    odd = place[0]
    copies = []
    for slot, (out, position) in enumerate(((first, layers - 1), (second, 0))):
        layer = layer_of(odd, position, layers)
        copies.append(pltpu.make_async_copy(dirs.at[:, layer], out.at[pl.ds(0, count)], sems.at[slot, 0]))
        copies.append(pltpu.make_async_copy(adj.at[layer], out.at[count], sems.at[slot, 1]))
    for copy in copies:
        copy.start()
    for copy in copies:
        copy.wait()


def coefficients_at(vel, dif, layer, half, sign, rows, first_row, last_row):
    spread = dif[layer, rows, :]
    ax = (half * sign) * vel[0, layer, rows, :]
    ay = half * vel[1, layer, rows, :]
    az = half * vel[2, layer, rows, :]
    up, down = spread + ay, spread - ay
    row = lax.broadcasted_iota(jnp.int32, spread.shape, 0)
    if last_row:
        up = jnp.where(row == spread.shape[0] - 1, 0.0, up)
    if first_row:
        down = jnp.where(row == 0, 0.0, down)
    return 1.0 - 6.0 * spread, spread + ax, spread - ax, up, down, spread + az, spread - az


def stencil(vel, dif, src, layer, half, sign, fields, rows_total, width, middle, toward, away, store):
    for base in range(0, rows_total, SUB):
        rows = slice(base, base + SUB)
        first_row, last_row = base == 0, base + SUB == rows_total
        c0, cxp, cxm, cyp, cym, czp, czm = coefficients_at(
            vel, dif, layer, half, sign, rows, first_row, last_row
        )
        for field in range(fields):
            tile = middle(field, rows)
            if last_row:
                above = pltpu.roll(tile, SUB - 1, 0)
            else:
                above = middle(field, slice(base + 1, base + 1 + SUB))
            if first_row:
                below = pltpu.roll(tile, 1, 0)
            else:
                below = middle(field, slice(base - 1, base - 1 + SUB))
            total = c0 * tile + cxp * toward(field, rows) + cxm * away(field, rows)
            total = total + (cyp * above + cym * below)
            total = total + (czp * pltpu.roll(tile, width - 1, 1) + czm * pltpu.roll(tile, 1, 1))
            if field == fields - 1:
                total = total + src[layer, rows, :]
            store(field, rows, total)


def reader(dirs, adj, count, layer):
    def read(field, rows):
        return dirs[field, layer, rows, :] if field < count else adj[layer, rows, :]

    return read


def plain(ref, *lead):
    def read(field, rows):
        return ref[(*lead, field, rows, slice(None))]

    return read


def writer(ref, *lead):
    def write(field, rows, value):
        ref[(*lead, field, rows, slice(None))] = value

    return write


def first_kernel(count, layers, place, half, dirs, adj, halo, vel, dif, src, edge, inner):
    odd, sign = place[0], (1 - 2 * place[0]).astype(jnp.float32)
    _, _, ny, nz = dirs.shape
    for position in range(layers - 1, 0, -1):
        layer = layer_of(odd, position, layers)
        last = position == layers - 1
        toward = plain(halo) if last else reader(dirs, adj, count, layer_of(odd, position + 1, layers))
        stencil(
            vel, dif, src, layer, half[0], sign, count + 1, ny, nz,
            reader(dirs, adj, count, layer), toward,
            reader(dirs, adj, count, layer_of(odd, position - 1, layers)),
            writer(edge) if last else writer(inner, position - 1),
        )


def second_kernel(count, layers, place, half, dirs, adj, halo, vel, dif, src, edge):
    odd, sign = place[0], (1 - 2 * place[0]).astype(jnp.float32)
    _, _, ny, nz = dirs.shape
    layer = layer_of(odd, 0, layers)
    stencil(
        vel, dif, src, layer, half[0], sign, count + 1, ny, nz,
        reader(dirs, adj, count, layer), reader(dirs, adj, count, layer_of(odd, 1, layers)), plain(halo),
        writer(edge),
    )


def add_products(ref, lead, count, ny, nz, total):
    step = 2 * SUB if ny % (2 * SUB) == 0 else SUB
    for base in range(0, ny, step):
        parts = [
            ref[(*lead, slice(None), slice(row, row + SUB), slice(None))].reshape((count + 1) * SUB, nz)
            for row in range(base, base + step, SUB)
        ]
        block = jnp.concatenate(parts, axis=1) if len(parts) > 1 else parts[0]
        total = total + lax.dot_general(
            block[: count * SUB], block, (((1,), (1,)), ((), ())),
            precision=HIGH, preferred_element_type=jnp.float32,
        )
    return total


def third_kernel(count, layers, place, half, bottom, inner, top, halo, vel, dif, src, out, products):
    odd, sign = place[0], (1 - 2 * place[0]).astype(jnp.float32)
    _, ny, nz = bottom.shape

    def at(position):
        if position == 0:
            return plain(bottom)
        if position == layers:
            return plain(halo)
        return plain(top) if position == layers - 1 else plain(inner, position - 1)

    total = jnp.zeros(products.shape, jnp.float32)
    for position in range(1, layers):
        layer = layer_of(odd, position, layers)
        stencil(
            vel, dif, src, layer, half[1], sign, count + 1, ny, nz,
            at(position), at(position + 1), at(position - 1), writer(out, position - 1),
        )
    for position in range(1, layers):
        total = add_products(out, (position - 1,), count, ny, nz, total)
    products[...] = total


def fourth_kernel(count, layers, place, half, bottom, above, halo, vel, dif, src, products, out, gram):
    odd, sign = place[0], (1 - 2 * place[0]).astype(jnp.float32)
    _, ny, nz = bottom.shape
    stencil(
        vel, dif, src, layer_of(odd, 0, layers), half[1], sign, count + 1, ny, nz,
        plain(bottom), plain(above), plain(halo), writer(out),
    )
    total = add_products(out, (), count, ny, nz, products[...])
    rows = lax.broadcasted_iota(jnp.int32, total.shape, 0)
    columns = lax.broadcasted_iota(jnp.int32, total.shape, 1)
    total = jnp.where(rows % SUB == columns % SUB, total, 0.0)
    total = total.reshape(count, SUB, total.shape[1]).sum(axis=1)
    width = gram.shape[1]
    gather = (
        lax.broadcasted_iota(jnp.int32, (total.shape[1], width), 0) // SUB
        == lax.broadcasted_iota(jnp.int32, (total.shape[1], width), 1)
    ).astype(jnp.float32)
    gram[...] = jnp.dot(total, gather, precision=HIGH, preferred_element_type=jnp.float32)


def solve_kernel(count, layers, pieces, cells, place, gram, upper, bottom, early, solved, shadow, *parts):
    odd, seg = place[0], place[1]
    _, ny, nz = bottom.shape
    shape = gram.shape
    row = lax.broadcasted_iota(jnp.int32, shape, 0)
    lane = lax.broadcasted_iota(jnp.int32, shape, 1)
    table = jnp.where(lane <= count, gram[...] / cells, 0.0)
    table = jnp.where(lane == row + count + 1, 1.0, table)
    for k in range(count):
        pivot_row = table[k : k + 1, :]
        root = jnp.sqrt(pivot_row[:, k : k + 1])
        scaled = pivot_row / root
        column = table[:, k : k + 1] / root
        table = jnp.where(row == k, scaled, jnp.where(row > k, table - column * scaled, table))
    table = jnp.where((lane < count) & (lane < row), 0.0, table)
    solved[...] = table
    weights = jnp.sum(table[:, count : count + 1] * table, axis=0, keepdims=True)
    splat = [
        jnp.broadcast_to(weights[:, count + 1 + j : count + 2 + j], (SUB, nz)) for j in range(count)
    ]
    for position in range(layers):
        layer = layer_of(odd, position, layers)
        read = plain(bottom) if position == 0 else plain(upper, position - 1)
        for base in range(0, ny, SUB):
            rows = slice(base, base + SUB)
            total = read(count, rows)
            for j in range(count):
                total = total - splat[j] * read(j, rows)
            shadow[layer, rows, :] = total
    step = ny // pieces
    for k, part in enumerate(parts):
        begin = pl.multiple_of((seg ^ k) * step, step)
        rows = pl.ds(begin, step)
        part[...] = shadow[:, rows, :] + early[:, rows, :]


def basis_kernel(count, layers, place, solved, upper, bottom, out):
    odd = place[0]
    _, ny, nz = bottom.shape
    block = min(ny, 8 * SUB)
    for position in range(layers):
        layer = layer_of(odd, position, layers)
        read = plain(bottom) if position == 0 else plain(upper, position - 1)
        for base in range(0, ny, block):
            rows = slice(base, base + block)
            for i in range(count):
                total = solved[i, count + 1] * read(0, rows)
                for j in range(1, i + 1):
                    total = total + solved[i, count + 1 + j] * read(j, rows)
                out[i, layer, rows, :] = total


def body(directions, adjoint, velocity, diffusivity, objective_source, segment_start):
    dirs, adj, vel, dif, src = (
        directions[0], adjoint[0], velocity[0], diffusivity[0], objective_source[0],
    )
    count, layers, ny, nz = dirs.shape
    spaces, segs = lax.axis_size("space"), lax.axis_size("seg")
    assert spaces % 2 == 0 and layers >= 2 and segs & (segs - 1) == 0 and spaces & (spaces - 1) == 0
    odd = lax.axis_index("space") % 2
    place = jnp.stack([odd, lax.axis_index("seg")]).astype(jnp.int32)
    half = jnp.stack([0.5 * modulation(segment_start[0], k) for k in (1, 2)])
    pair_one = [(i, i ^ 1) for i in range(spaces)]
    pair_two = [(i, (i + 1) % spaces if i % 2 else (i - 1) % spaces) for i in range(spaces)]
    f32 = functools.partial(jax.ShapeDtypeStruct, dtype=jnp.float32)
    edge = f32((count + 1, ny, nz))
    field_bytes = 4 * (count + 1) * ny * nz
    vs, ss = VMEM_SPEC, SMEM_SPEC

    send_one, send_two = call(
        functools.partial(pack_kernel, count, layers), "pack", [edge, edge],
        [ss, ANY_SPEC, ANY_SPEC], (place, dirs, adj),
        scratch=[pltpu.SemaphoreType.DMA((2, 2))], moved=4 * field_bytes,
    )
    halo_one = lax.ppermute(send_one, "space", pair_one)
    halo_two = lax.ppermute(send_two, "space", pair_two)
    top, inner = call(
        functools.partial(first_kernel, count, layers), "first",
        [edge, f32((max(layers - 2, 1), count + 1, ny, nz))],
        [ss, ss, vs, vs, vs, vs, vs, vs], (place, half, dirs, adj, halo_one, vel, dif, src),
        flops=13 * layers * field_bytes // 4, moved=2 * layers * field_bytes,
    )
    next_one = lax.ppermute(top, "space", pair_one)
    bottom = call(
        functools.partial(second_kernel, count, layers), "second", edge,
        [ss, ss, vs, vs, vs, vs, vs, vs], (place, half, dirs, adj, halo_two, vel, dif, src),
        flops=13 * field_bytes // 4, moved=layers * field_bytes,
    )
    next_two = lax.ppermute(bottom, "space", pair_two)
    products_shape = f32((count * SUB, (count + 1) * SUB))
    upper, products = call(
        functools.partial(third_kernel, count, layers), "third",
        [f32((layers - 1, count + 1, ny, nz)), products_shape],
        [ss, ss] + [vs] * 7, (place, half, bottom, inner, top, next_one, vel, dif, src),
        flops=60 * layers * field_bytes // 4, moved=2 * layers * field_bytes,
    )
    lowest, gram = call(
        functools.partial(fourth_kernel, count, layers), "fourth", [edge, f32((count, 128))],
        [ss, ss] + [vs] * 7,
        (place, half, bottom, inner[0] if layers > 2 else top, next_two, vel, dif, src, products),
        flops=60 * field_bytes // 4, moved=4 * field_bytes,
    )
    reach = 1
    while reach < spaces:
        gram = gram + lax.ppermute(gram, "space", [(i, i ^ reach) for i in range(spaces)])
        reach *= 2
    early_layers = [top[count]]
    early_layers = [bottom[count]] + [inner[p, count] for p in range(layers - 2)] + early_layers
    early = jnp.stack(early_layers)
    early = jnp.where(odd == 1, early[::-1], early)
    piece = f32((layers, ny // segs, nz))
    solved, shadow, *parts = call(
        functools.partial(solve_kernel, count, layers, segs, float(layers * ny * nz * spaces)), "solve",
        [f32((count, 128)), f32((layers, ny, nz))] + [piece] * segs,
        [ss] + [vs] * 4, (place, gram, upper, lowest, early),
        flops=2 * layers * field_bytes, moved=layers * field_bytes,
    )
    gradient = parts[0]
    for k in range(1, segs):
        gradient = gradient + lax.ppermute(parts[k], "seg", [(i, i ^ k) for i in range(segs)])
    basis = call(
        functools.partial(basis_kernel, count, layers), "basis", f32((count, layers, ny, nz)),
        [ss, ss, vs, vs], (place, solved, upper, lowest),
        flops=count * layers * field_bytes // 4, moved=2 * layers * field_bytes,
    )
    return (
        basis[None], solved[None, :, :count], solved[None, :, count], shadow[None], gradient,
    )


def solution(mesh):
    return jax.shard_map(
        body,
        mesh=mesh,
        in_specs=(
            P("seg", None, "space", None, None),
            P("seg", "space", None, None),
            P("seg", None, "space", None, None),
            P("seg", "space", None, None),
            P("seg", "space", None, None),
            P("seg"),
        ),
        out_specs=(
            P("seg", None, "space", None, None),
            P("seg", None, None),
            P("seg", None),
            P("seg", "space", None, None),
            P("space", "seg", None),
        ),
        check_vma=False,
    )
```

```python
import functools
import math

import jax
import jax.numpy as jnp
from jax import lax
from jax.experimental import pallas as pl
from jax.experimental.pallas import tpu as pltpu
from jax.sharding import PartitionSpec as P


SUB = 8
HIGH = lax.Precision.HIGHEST
VMEM_SPEC = pl.BlockSpec(memory_space=pltpu.VMEM)
SMEM_SPEC = pl.BlockSpec(memory_space=pltpu.SMEM)
ANY_SPEC = pl.BlockSpec(memory_space=pl.ANY)
HBM_SPEC = pl.BlockSpec(memory_space=pltpu.HBM)


def modulation(window_start, section):
    phase_step = (window_start + 2 - section) % 64
    return 1.0 + 0.5 * jnp.sin(2.0 * math.pi * phase_step.astype(jnp.float32) / 64.0)


def call(body, outs, specs, args, scratch=(), flops=0, moved=0):
    return pl.pallas_call(
        body,
        out_shape=outs,
        in_specs=specs,
        out_specs=jax.tree.map(lambda _: VMEM_SPEC, outs),
        scratch_shapes=scratch,
        cost_estimate=pl.CostEstimate(flops=flops, transcendentals=0, bytes_accessed=moved),
        compiler_params=pltpu.CompilerParams(vmem_limit_bytes=20 * 1024 * 1024),
    )(*args)


def layer_of(odd, position, layers):
    return position + odd * (layers - 1 - 2 * position)


def pack_kernel(count, layers, positions, cuts, place, dirs, adj, *rest):
    outs, sems = rest[:-1], rest[-1]
    odd = place[0]
    copies = []
    for k, (out, position) in enumerate(zip(outs, positions)):
        layer = layer_of(odd, position, layers)
        stop = min(cuts[k + 1], count)
        size = stop - cuts[k]
        copies.append(
            pltpu.make_async_copy(dirs.at[pl.ds(cuts[k], size), layer], out.at[pl.ds(0, size)], sems.at[k])
        )
        if cuts[k + 1] > count:
            copies.append(pltpu.make_async_copy(adj.at[layer], out.at[size], sems.at[2]))
    for copy in copies:
        copy.start()
    for copy in copies:
        copy.wait()


def coefficients_at(vel, dif, layer, half, sign, rows, first_row, last_row):
    spread = dif[layer, rows, :]
    ax = (half * sign) * vel[0, layer, rows, :]
    ay = half * vel[1, layer, rows, :]
    az = half * vel[2, layer, rows, :]
    up, down = spread + ay, spread - ay
    row = lax.broadcasted_iota(jnp.int32, spread.shape, 0)
    if last_row:
        up = jnp.where(row == spread.shape[0] - 1, 0.0, up)
    if first_row:
        down = jnp.where(row == 0, 0.0, down)
    return 1.0 - 6.0 * spread, spread + ax, spread - ax, up, down, spread + az, spread - az


def stencil(
    vel, dif, src, layer, half, sign, fields, count, rows_total, width, middle, toward, away, store
):
    for base in range(0, rows_total, SUB):
        rows = slice(base, base + SUB)
        first_row, last_row = base == 0, base + SUB == rows_total
        c0, cxp, cxm, cyp, cym, czp, czm = coefficients_at(
            vel, dif, layer, half, sign, rows, first_row, last_row
        )
        for field in fields:
            tile = middle(field, rows)
            if last_row:
                above = pltpu.roll(tile, SUB - 1, 0)
            else:
                above = middle(field, slice(base + 1, base + 1 + SUB))
            if first_row:
                below = pltpu.roll(tile, 1, 0)
            else:
                below = middle(field, slice(base - 1, base - 1 + SUB))
            total = c0 * tile + cxp * toward(field, rows) + cxm * away(field, rows)
            total = total + (cyp * above + cym * below)
            total = total + (czp * pltpu.roll(tile, width - 1, 1) + czm * pltpu.roll(tile, 1, 1))
            if field == count:
                total = total + src[layer, rows, :]
            store(field, rows, total)


def reader(dirs, adj, count, layer):
    def read(field, rows):
        return dirs[field, layer, rows, :] if field < count else adj[layer, rows, :]

    return read


def plain(ref, *lead):
    def read(field, rows):
        return ref[(*lead, field, rows, slice(None))]

    return read


def joined(first, second):
    cut = first.shape[0]

    def read(field, rows):
        return first[field, rows, :] if field < cut else second[field - cut, rows, :]

    return read


def writer(ref, *lead, start=0):
    def write(field, rows, value):
        ref[(*lead, field - start, rows, slice(None))] = value

    return write


def sign_of(place):
    return (1 - 2 * place[0]).astype(jnp.float32)


def inner_kernel(count, layers, place, half, dirs, adj, vel, dif, src, inner):
    odd = place[0]
    _, _, ny, nz = dirs.shape
    for position in range(1, layers - 1):
        near, here, far = (layer_of(odd, position + k, layers) for k in (1, 0, -1))
        stencil(
            vel, dif, src, here, half[0], sign_of(place), range(count + 1), count, ny, nz,
            reader(dirs, adj, count, here), reader(dirs, adj, count, near), reader(dirs, adj, count, far),
            writer(inner, position - 1),
        )


def bottom_kernel(count, layers, place, half, dirs, adj, halo, vel, dif, src, edge):
    odd = place[0]
    _, _, ny, nz = dirs.shape
    here, near = layer_of(odd, 0, layers), layer_of(odd, 1, layers)
    stencil(
        vel, dif, src, here, half[0], sign_of(place), range(count + 1), count, ny, nz,
        reader(dirs, adj, count, here), reader(dirs, adj, count, near), plain(halo), writer(edge),
    )


def top_kernel(count, layers, start, place, half, dirs, adj, halo, vel, dif, src, order, edge):
    odd = place[0]
    _, _, ny, nz = dirs.shape
    here, far = layer_of(odd, layers - 1, layers), layer_of(odd, layers - 2, layers)

    def toward(field, rows):
        return halo[field - start, rows, :]

    stencil(
        vel, dif, src, here, half[0], sign_of(place), range(start, start + edge.shape[0]), count, ny, nz,
        reader(dirs, adj, count, here), toward, reader(dirs, adj, count, far), writer(edge, start=start),
    )


def add_products(tiles, count, ny, total):
    step = 2 * SUB if ny % (2 * SUB) == 0 else SUB
    for base in range(0, ny, step):
        parts = [tiles(slice(row, row + SUB)) for row in range(base, base + step, SUB)]
        block = jnp.concatenate(parts, axis=1) if len(parts) > 1 else parts[0]
        total = total + lax.dot_general(
            block[: count * SUB], block, (((1,), (1,)), ((), ())),
            precision=HIGH, preferred_element_type=jnp.float32,
        )
    return total


def flat(tile):
    return tile.reshape(tile.shape[0] * tile.shape[1], tile.shape[2])


def middle_kernel(
    count, layers, place, half, bottom, inner, top_a, top_b, vel, dif, src, out, products, early
):
    odd = place[0]
    _, ny, nz = bottom.shape

    def at(position):
        if position == 0:
            return plain(bottom)
        return joined(top_a, top_b) if position == layers - 1 else plain(inner, position - 1)

    for position in range(1, layers - 1):
        stencil(
            vel, dif, src, layer_of(odd, position, layers), half[1], sign_of(place), range(count + 1),
            count, ny, nz, at(position), at(position + 1), at(position - 1), writer(out, position - 1),
        )
    for position in range(layers):
        early[layer_of(odd, position, layers)] = at(position)(count, slice(0, ny))
    total = jnp.zeros(products.shape, jnp.float32)
    for position in range(1, layers - 1):
        total = add_products(lambda rows: flat(out[position - 1, :, rows, :]), count, ny, total)
    products[...] = total


def low_kernel(count, layers, place, half, bottom, inner, halo, vel, dif, src, before, out, products):
    odd = place[0]
    _, ny, nz = bottom.shape
    stencil(
        vel, dif, src, layer_of(odd, 0, layers), half[1], sign_of(place), range(count + 1), count, ny, nz,
        plain(bottom), plain(inner, 0), plain(halo), writer(out),
    )
    products[...] = add_products(lambda rows: flat(out[:, rows, :]), count, ny, before[...])


def high_stencil(count, layers, start, place, half, top, inner, halo, vel, dif, src, out):
    _, ny, nz = top.shape

    def middle(field, rows):
        return top[field - start, rows, :]

    def toward(field, rows):
        return halo[field - start, rows, :]

    stencil(
        vel, dif, src, layer_of(place[0], layers - 1, layers), half[1], sign_of(place),
        range(start, start + out.shape[0]), count, ny, nz, middle, toward, plain(inner, layers - 3),
        writer(out, start=start),
    )


def high_a_kernel(count, layers, place, half, top, inner, halo, vel, dif, src, order, out):
    high_stencil(count, layers, 0, place, half, top, inner, halo, vel, dif, src, out)


def high_b_kernel(
    count, layers, place, half, top, inner, halo, vel, dif, src, before, out_a, out, gram
):
    start = out_a.shape[0]
    _, ny, _ = top.shape
    high_stencil(count, layers, start, place, half, top, inner, halo, vel, dif, src, out)
    total = add_products(
        lambda rows: jnp.concatenate([flat(out_a[:, rows, :]), flat(out[:, rows, :])], axis=0),
        count, ny, before[...],
    )
    rows = lax.broadcasted_iota(jnp.int32, total.shape, 0)
    columns = lax.broadcasted_iota(jnp.int32, total.shape, 1)
    total = jnp.where(rows % SUB == columns % SUB, total, 0.0)
    total = total.reshape(count, SUB, total.shape[1]).sum(axis=1)
    width = gram.shape[1]
    gather = (
        lax.broadcasted_iota(jnp.int32, (total.shape[1], width), 0) // SUB
        == lax.broadcasted_iota(jnp.int32, (total.shape[1], width), 1)
    ).astype(jnp.float32)
    gram[...] = jnp.dot(total, gather, precision=HIGH, preferred_element_type=jnp.float32)


def result_at(position, layers, low, mid, high_a, high_b):
    if position == 0:
        return plain(low)
    return joined(high_a, high_b) if position == layers - 1 else plain(mid, position - 1)


def solve_kernel(
    count, layers, pieces, cells, place, gram, low, mid, high_a, high_b, early,
    solved, factor, along, shadow, *parts,
):
    odd, seg = place[0], place[1]
    _, ny, nz = low.shape
    shape = gram.shape
    row = lax.broadcasted_iota(jnp.int32, shape, 0)
    lane = lax.broadcasted_iota(jnp.int32, shape, 1)
    table = jnp.where(lane <= count, gram[...] / cells, 0.0)
    table = jnp.where(lane == row + count + 1, 1.0, table)
    for k in range(count):
        pivot_row = table[k : k + 1, :]
        root = jnp.sqrt(pivot_row[:, k : k + 1])
        scaled = pivot_row / root
        column = table[:, k : k + 1] / root
        table = jnp.where(row == k, scaled, jnp.where(row > k, table - column * scaled, table))
    table = jnp.where((lane < count) & (lane < row), 0.0, table)
    solved[...] = table
    weights = jnp.sum(table[:, count : count + 1] * table, axis=0, keepdims=True)
    splat = [
        jnp.broadcast_to(weights[:, count + 1 + j : count + 2 + j], (SUB, nz)) for j in range(count)
    ]
    for position in range(layers):
        layer = layer_of(odd, position, layers)
        read = result_at(position, layers, low, mid, high_a, high_b)
        for base in range(0, ny, SUB):
            rows = slice(base, base + SUB)
            total = read(count, rows)
            for j in range(count):
                total = total - splat[j] * read(j, rows)
            shadow[layer, rows, :] = total
    step = ny // pieces
    for k, part in enumerate(parts):
        begin = pl.multiple_of((seg ^ k) * step, step)
        rows = pl.ds(begin, step)
        part[...] = shadow[:, rows, :] + early[:, rows, :]
    factor[...] = table[:, :count]
    eye = (
        lax.broadcasted_iota(jnp.int32, (count, count), 0) == lax.broadcasted_iota(jnp.int32, (count, count), 1)
    )
    along[...] = jnp.sum(jnp.where(eye, table[:, count : count + 1], 0.0), axis=0, keepdims=True)


def basis_kernel(count, layers, place, solved, low, mid, high_a, high_b, out):
    odd = place[0]
    _, ny, _ = low.shape
    block = min(ny, 8 * SUB)
    for position in range(layers):
        layer = layer_of(odd, position, layers)
        read = result_at(position, layers, low, mid, high_a, high_b)
        for base in range(0, ny, block):
            rows = slice(base, base + block)
            for i in range(count):
                total = solved[i, count + 1] * read(0, rows)
                for j in range(1, i + 1):
                    total = total + solved[i, count + 1 + j] * read(j, rows)
                out[i, layer, rows, :] = total


def window(directions, adjoint, velocity, diffusivity, objective_source, segment_start):
    dirs, adj, vel, dif, src = (
        directions[0], adjoint[0], velocity[0], diffusivity[0], objective_source[0],
    )
    count, layers, ny, nz = dirs.shape
    fields, part_a = count + 1, (count + 2) // 2
    spaces, segs = lax.axis_size("space"), lax.axis_size("seg")
    assert spaces & (spaces - 1) == 0 and segs & (segs - 1) == 0 and layers >= 3
    odd = lax.axis_index("space") % 2
    place = jnp.stack([odd, lax.axis_index("seg")]).astype(jnp.int32)
    half = jnp.stack([0.5 * modulation(segment_start[0], k) for k in (1, 2)])
    pair_one = [(i, i ^ 1) for i in range(spaces)]
    pair_two = [(i, (i + 1) % spaces if i % 2 else (i - 1) % spaces) for i in range(spaces)]
    f32 = functools.partial(jax.ShapeDtypeStruct, dtype=jnp.float32)
    edge, edge_a, edge_b = (f32((n, ny, nz)) for n in (fields, part_a, fields - part_a))
    layer_bytes = 4 * fields * ny * nz
    layer_flops = 13 * fields * ny * nz
    vs, ss, hs, anys = VMEM_SPEC, SMEM_SPEC, HBM_SPEC, ANY_SPEC
    flow = (vel, dif, src)

    dirs_hbm, adj_hbm = (pltpu.with_memory_space_constraint(x, pltpu.HBM) for x in (dirs, adj))
    near_a, near_b = call(
        functools.partial(pack_kernel, count, layers, (layers - 1, layers - 1), (0, part_a, fields)),
        [edge_a, edge_b], [ss, hs, hs], (place, dirs_hbm, adj_hbm),
        scratch=[pltpu.SemaphoreType.DMA((3,))], moved=2 * layer_bytes,
    )
    halo_a = lax.ppermute(near_a, "space", pair_one)
    halo_b = lax.ppermute(near_b, "space", pair_one)
    (far,) = call(
        functools.partial(pack_kernel, count, layers, (0,), (0, fields)),
        [edge], [ss, hs, hs], (place, dirs_hbm, adj_hbm),
        scratch=[pltpu.SemaphoreType.DMA((3,))], moved=2 * layer_bytes,
    )
    halo_far = lax.ppermute(far, "space", pair_two)
    inner = call(
        functools.partial(inner_kernel, count, layers), f32((layers - 2, fields, ny, nz)),
        [ss, ss] + [vs] * 5, (place, half, dirs, adj) + flow,
        flops=(layers - 2) * layer_flops, moved=6 * layer_bytes,
    )
    bottom = call(
        functools.partial(bottom_kernel, count, layers), edge,
        [ss, ss] + [vs] * 6, (place, half, dirs, adj, halo_far) + flow,
        flops=layer_flops, moved=4 * layer_bytes,
    )
    bottom_far = lax.ppermute(bottom, "space", pair_two)
    top_a = call(
        functools.partial(top_kernel, count, layers, 0), edge_a,
        [ss, ss] + [vs] * 6 + [anys], (place, half, dirs, adj, halo_a) + flow + (bottom,),
        flops=layer_flops // 2, moved=2 * layer_bytes,
    )
    near_top_a = lax.ppermute(top_a, "space", pair_one)
    top_b = call(
        functools.partial(top_kernel, count, layers, part_a), edge_b,
        [ss, ss] + [vs] * 6 + [anys], (place, half, dirs, adj, halo_b) + flow + (top_a,),
        flops=layer_flops // 2, moved=2 * layer_bytes,
    )
    near_top_b = lax.ppermute(top_b, "space", pair_one)
    mid, products, early = call(
        functools.partial(middle_kernel, count, layers),
        [f32((layers - 2, fields, ny, nz)), f32((count * SUB, fields * SUB)), f32((layers, ny, nz))],
        [ss, ss] + [vs] * 7, (place, half, bottom, inner, top_a, top_b) + flow,
        flops=4 * (layers - 2) * layer_flops, moved=6 * layer_bytes,
    )
    low, products = call(
        functools.partial(low_kernel, count, layers), [edge, f32((count * SUB, fields * SUB))],
        [ss, ss] + [vs] * 7, (place, half, bottom, inner, bottom_far) + flow + (products,),
        flops=4 * layer_flops, moved=4 * layer_bytes,
    )
    high_a = call(
        functools.partial(high_a_kernel, count, layers), edge_a,
        [ss, ss] + [vs] * 6 + [anys], (place, half, top_a, inner, near_top_a) + flow + (low,),
        flops=layer_flops // 2, moved=2 * layer_bytes,
    )
    high_b, gram = call(
        functools.partial(high_b_kernel, count, layers), [edge_b, f32((count, 128))],
        [ss, ss] + [vs] * 8, (place, half, top_b, inner, near_top_b) + flow + (products, high_a),
        flops=2 * layer_flops, moved=2 * layer_bytes,
    )
    reach = 1
    while reach < spaces:
        gram = gram + lax.ppermute(gram, "space", [(i, i ^ reach) for i in range(spaces)])
        reach *= 2
    piece = f32((layers, ny // segs, nz))
    solved, factor, along, shadow, *parts = call(
        functools.partial(solve_kernel, count, layers, segs, float(layers * ny * nz * spaces)),
        [f32((count, 128)), f32((count, count)), f32((1, count)), f32((layers, ny, nz))] + [piece] * segs,
        [ss] + [vs] * 6, (place, gram, low, mid, high_a, high_b, early),
        flops=4 * layer_flops, moved=4 * layer_bytes,
    )
    gradient = parts[0]
    for k in range(1, segs):
        gradient = gradient + lax.ppermute(parts[k], "seg", [(i, i ^ k) for i in range(segs)])
    basis = call(
        functools.partial(basis_kernel, count, layers), f32((count, layers, ny, nz)),
        [ss, ss] + [vs] * 4, (place, solved, low, mid, high_a, high_b),
        flops=8 * layer_flops, moved=8 * layer_bytes,
    )
    return basis[None], factor[None], along, shadow[None], gradient


def solution(mesh):
    return jax.shard_map(
        window,
        mesh=mesh,
        in_specs=(
            P("seg", None, "space", None, None),
            P("seg", "space", None, None),
            P("seg", None, "space", None, None),
            P("seg", "space", None, None),
            P("seg", "space", None, None),
            P("seg"),
        ),
        out_specs=(
            P("seg", None, "space", None, None),
            P("seg", None, None),
            P("seg", None),
            P("seg", "space", None, None),
            P("space", "seg", None),
        ),
        check_vma=False,
    )
```

```python
import functools
import math

import jax
import jax.numpy as jnp
from jax import lax
from jax.experimental import pallas as pl
from jax.experimental.pallas import tpu as pltpu
from jax.sharding import PartitionSpec as P


SUB = 8
TURNS = 800
HIGH = lax.Precision.HIGHEST
VMEM_SPEC = pl.BlockSpec(memory_space=pltpu.VMEM)
SMEM_SPEC = pl.BlockSpec(memory_space=pltpu.SMEM)
ANY_SPEC = pl.BlockSpec(memory_space=pl.ANY)
HBM_SPEC = pl.BlockSpec(memory_space=pltpu.HBM)


def modulation(window_start, section):
    phase_step = (window_start + 2 - section) % 64
    return 1.0 + 0.5 * jnp.sin(2.0 * math.pi * phase_step.astype(jnp.float32) / 64.0)


def call(body, outs, specs, args, scratch=(), flops=0, moved=0, out_specs=None, grant=16):
    return pl.pallas_call(
        body,
        out_shape=outs,
        in_specs=specs,
        out_specs=out_specs or jax.tree.map(lambda _: VMEM_SPEC, outs),
        scratch_shapes=scratch,
        cost_estimate=pl.CostEstimate(flops=flops, transcendentals=0, bytes_accessed=moved),
        compiler_params=pltpu.CompilerParams(vmem_limit_bytes=grant * 1024 * 1024),
    )(*args)


def layer_of(odd, position, layers):
    return position + odd * (layers - 1 - 2 * position)


def pack_kernel(count, layers, position, start, stop, place, dirs, adj, out, sems):
    layer = layer_of(place[0], position, layers)
    size = min(stop, count) - start
    copies = [
        pltpu.make_async_copy(dirs.at[pl.ds(start, size), layer], out.at[pl.ds(0, size)], sems.at[0])
    ]
    if stop > count:
        copies.append(pltpu.make_async_copy(adj.at[layer], out.at[size], sems.at[1]))
    for copy in copies:
        copy.start()
    for copy in copies:
        copy.wait()


def pack_both(count, layers, position, cut, place, dirs, adj, first, second, sems):
    layer = layer_of(place[0], position, layers)
    copies = [
        pltpu.make_async_copy(dirs.at[pl.ds(0, cut), layer], first, sems.at[0]),
        pltpu.make_async_copy(
            dirs.at[pl.ds(cut, count - cut), layer], second.at[pl.ds(0, count - cut)], sems.at[1]
        ),
        pltpu.make_async_copy(adj.at[layer], second.at[count - cut], sems.at[2]),
    ]
    for copy in copies:
        copy.start()
    for copy in copies:
        copy.wait()


def coefficients_at(vel, dif, layer, half, sign, rows, first_row, last_row):
    spread = dif[layer, rows, :]
    ax = (half * sign) * vel[0, layer, rows, :]
    ay = half * vel[1, layer, rows, :]
    az = half * vel[2, layer, rows, :]
    up, down = spread + ay, spread - ay
    row = lax.broadcasted_iota(jnp.int32, spread.shape, 0)
    if last_row:
        up = jnp.where(row == spread.shape[0] - 1, 0.0, up)
    if first_row:
        down = jnp.where(row == 0, 0.0, down)
    return 1.0 - 6.0 * spread, spread + ax, spread - ax, up, down, spread + az, spread - az


def stencil(
    vel, dif, src, layer, half, sign, fields, count, rows_total, width, middle, toward, away, store
):
    for base in range(0, rows_total, SUB):
        rows = slice(base, base + SUB)
        first_row, last_row = base == 0, base + SUB == rows_total
        c0, cxp, cxm, cyp, cym, czp, czm = coefficients_at(
            vel, dif, layer, half, sign, rows, first_row, last_row
        )
        for field in fields:
            tile = middle(field, rows)
            if last_row:
                above = pltpu.roll(tile, SUB - 1, 0)
            else:
                above = middle(field, slice(base + 1, base + 1 + SUB))
            if first_row:
                below = pltpu.roll(tile, 1, 0)
            else:
                below = middle(field, slice(base - 1, base - 1 + SUB))
            total = c0 * tile + cxp * toward(field, rows) + cxm * away(field, rows)
            total = total + (cyp * above + cym * below)
            total = total + (czp * pltpu.roll(tile, width - 1, 1) + czm * pltpu.roll(tile, 1, 1))
            if field == count:
                total = total + src[layer, rows, :]
            store(field, rows, total)


def reader(dirs, adj, count, layer):
    def read(field, rows):
        return dirs[field, layer, rows, :] if field < count else adj[layer, rows, :]

    return read


def plain(ref, *lead):
    def read(field, rows):
        return ref[(*lead, field, rows, slice(None))]

    return read


def joined(first, second):
    cut = first.shape[0]

    def read(field, rows):
        return first[field, rows, :] if field < cut else second[field - cut, rows, :]

    return read


def writer(ref, *lead, start=0):
    def write(field, rows, value):
        ref[(*lead, field - start, rows, slice(None))] = value

    return write


def sign_of(place):
    return (1 - 2 * place[0]).astype(jnp.float32)


def inner_kernel(count, layers, place, half, dirs, adj, vel, dif, src, inner):
    odd = place[0]
    _, _, ny, nz = dirs.shape
    for position in range(1, layers - 1):
        near, here, far = (layer_of(odd, position + k, layers) for k in (1, 0, -1))
        stencil(
            vel, dif, src, here, half[0], sign_of(place), range(count + 1), count, ny, nz,
            reader(dirs, adj, count, here), reader(dirs, adj, count, near), reader(dirs, adj, count, far),
            writer(inner, position - 1),
        )


def bottom_kernel(count, layers, place, half, dirs, adj, halo, vel, dif, src, edge):
    odd = place[0]
    _, _, ny, nz = dirs.shape
    here, near = layer_of(odd, 0, layers), layer_of(odd, 1, layers)
    stencil(
        vel, dif, src, here, half[0], sign_of(place), range(count + 1), count, ny, nz,
        reader(dirs, adj, count, here), reader(dirs, adj, count, near), plain(halo), writer(edge),
    )


def top_kernel(
    count, layers, start, turns, place, half, dirs, adj, halo, vel, dif, src, order, edge, turned
):
    def turn(step, total):
        turned[0] = turned[0] + step
        return total

    turned[0] = 0
    lax.fori_loop(0, turns * (place[1] % 2), turn, 0)
    odd = place[0]
    _, _, ny, nz = dirs.shape
    here, far = layer_of(odd, layers - 1, layers), layer_of(odd, layers - 2, layers)

    def toward(field, rows):
        return halo[field - start, rows, :]

    stencil(
        vel, dif, src, here, half[0], sign_of(place), range(start, start + edge.shape[0]), count, ny, nz,
        reader(dirs, adj, count, here), toward, reader(dirs, adj, count, far), writer(edge, start=start),
    )


def add_products(tiles, count, ny, total):
    step = 2 * SUB if ny % (2 * SUB) == 0 else SUB
    for base in range(0, ny, step):
        parts = [tiles(slice(row, row + SUB)) for row in range(base, base + step, SUB)]
        block = jnp.concatenate(parts, axis=1) if len(parts) > 1 else parts[0]
        total = total + lax.dot_general(
            block[: count * SUB], block, (((1,), (1,)), ((), ())),
            precision=HIGH, preferred_element_type=jnp.float32,
        )
    return total


def flat(tile):
    return tile.reshape(tile.shape[0] * tile.shape[1], tile.shape[2])


def middle_kernel(
    count, layers, place, half, bottom, inner, top_a, top_b, vel, dif, src, out, products, early
):
    odd = place[0]
    _, ny, nz = bottom.shape

    def at(position):
        if position == 0:
            return plain(bottom)
        return joined(top_a, top_b) if position == layers - 1 else plain(inner, position - 1)

    for position in range(1, layers - 1):
        stencil(
            vel, dif, src, layer_of(odd, position, layers), half[1], sign_of(place), range(count + 1),
            count, ny, nz, at(position), at(position + 1), at(position - 1), writer(out, position - 1),
        )
    for position in range(layers):
        early[layer_of(odd, position, layers)] = at(position)(count, slice(0, ny))
    total = jnp.zeros(products.shape, jnp.float32)
    for position in range(1, layers - 1):
        total = add_products(lambda rows: flat(out[position - 1, :, rows, :]), count, ny, total)
    products[...] = total


def low_kernel(count, layers, place, half, bottom, inner, halo, vel, dif, src, before, out, products):
    odd = place[0]
    _, ny, nz = bottom.shape
    stencil(
        vel, dif, src, layer_of(odd, 0, layers), half[1], sign_of(place), range(count + 1), count, ny, nz,
        plain(bottom), plain(inner, 0), plain(halo), writer(out),
    )
    products[...] = add_products(lambda rows: flat(out[:, rows, :]), count, ny, before[...])


def high_stencil(count, layers, start, place, half, top, inner, halo, vel, dif, src, out):
    _, ny, nz = top.shape

    def middle(field, rows):
        return top[field - start, rows, :]

    def toward(field, rows):
        return halo[field - start, rows, :]

    stencil(
        vel, dif, src, layer_of(place[0], layers - 1, layers), half[1], sign_of(place),
        range(start, start + out.shape[0]), count, ny, nz, middle, toward, plain(inner, layers - 3),
        writer(out, start=start),
    )


def high_a_kernel(count, layers, place, half, top, inner, halo, vel, dif, src, order, out):
    high_stencil(count, layers, 0, place, half, top, inner, halo, vel, dif, src, out)


def high_b_kernel(
    count, layers, place, half, top, inner, halo, vel, dif, src, before, out_a, out, gram
):
    start = out_a.shape[0]
    _, ny, _ = top.shape
    high_stencil(count, layers, start, place, half, top, inner, halo, vel, dif, src, out)
    total = add_products(
        lambda rows: jnp.concatenate([flat(out_a[:, rows, :]), flat(out[:, rows, :])], axis=0),
        count, ny, before[...],
    )
    rows = lax.broadcasted_iota(jnp.int32, total.shape, 0)
    columns = lax.broadcasted_iota(jnp.int32, total.shape, 1)
    total = jnp.where(rows % SUB == columns % SUB, total, 0.0)
    total = total.reshape(count, SUB, total.shape[1]).sum(axis=1)
    width = gram.shape[1]
    gather = (
        lax.broadcasted_iota(jnp.int32, (total.shape[1], width), 0) // SUB
        == lax.broadcasted_iota(jnp.int32, (total.shape[1], width), 1)
    ).astype(jnp.float32)
    gram[...] = jnp.dot(total, gather, precision=HIGH, preferred_element_type=jnp.float32)


def result_at(position, layers, low, mid, high_a, high_b):
    if position == 0:
        return plain(low)
    return joined(high_a, high_b) if position == layers - 1 else plain(mid, position - 1)


def solve_kernel(
    count, layers, pieces, cells, place, gram, low, mid, high_a, high_b, early, solved, shadow, *parts
):
    odd, seg = place[0], place[1]
    _, ny, nz = low.shape
    shape = gram.shape
    row = lax.broadcasted_iota(jnp.int32, shape, 0)
    lane = lax.broadcasted_iota(jnp.int32, shape, 1)
    table = jnp.where(lane <= count, gram[...] / cells, 0.0)
    table = jnp.where(lane == row + count + 1, 1.0, table)
    scale = jnp.ones(shape, jnp.float32)
    columns = [jnp.broadcast_to(table[:, j : j + 1], shape) for j in range(count)]
    for k in range(count):
        pivot = jnp.broadcast_to(columns[k][k : k + 1, :], shape)
        scale = jnp.where(row == k, pivot, scale)
        ratio = jnp.where(row > k, columns[k] * (1.0 / pivot), 0.0)
        for j in range(k + 1, count):
            columns[j] = columns[j] - ratio * jnp.broadcast_to(columns[j][k : k + 1, :], shape)
        table = table - ratio * jnp.broadcast_to(table[k : k + 1, :], shape)
    table = table / jnp.sqrt(scale)
    table = jnp.where((lane < count) & (lane < row), 0.0, table)
    solved[...] = table
    weights = jnp.sum(table[:, count : count + 1] * table, axis=0, keepdims=True)
    splat = [
        jnp.broadcast_to(weights[:, count + 1 + j : count + 2 + j], (SUB, nz)) for j in range(count)
    ]
    for position in range(layers):
        layer = layer_of(odd, position, layers)
        read = result_at(position, layers, low, mid, high_a, high_b)
        for base in range(0, ny, SUB):
            rows = slice(base, base + SUB)
            total = read(count, rows)
            for j in range(count):
                total = total - splat[j] * read(j, rows)
            shadow[layer, rows, :] = total
    step = ny // pieces
    for k, part in enumerate(parts):
        begin = pl.multiple_of((seg ^ k) * step, step)
        rows = pl.ds(begin, step)
        part[...] = shadow[:, rows, :] + early[:, rows, :]


def basis_kernel(
    count, layers, place, weights, solved, shadow, low, mid, high_a, high_b,
    out, factor, along, shadow_out, held, sems,
):
    odd = place[0]
    _, ny, _ = low.shape
    block = min(ny, 8 * SUB)
    copies = [pltpu.make_async_copy(shadow, shadow_out, sems.at[count])]
    copies[0].start()
    table = solved[...]
    factor[...] = table[:, :count]
    eye = (
        lax.broadcasted_iota(jnp.int32, (count, count), 0) == lax.broadcasted_iota(jnp.int32, (count, count), 1)
    )
    along[...] = jnp.sum(jnp.where(eye, table[:, count : count + 1], 0.0), axis=0, keepdims=True)
    for i in range(count):
        for position in range(layers):
            layer = layer_of(odd, position, layers)
            read = result_at(position, layers, low, mid, high_a, high_b)
            for base in range(0, ny, block):
                rows = slice(base, base + block)
                total = weights[i, count + 1] * read(0, rows)
                for j in range(1, i + 1):
                    total = total + weights[i, count + 1 + j] * read(j, rows)
                held[i, layer, rows, :] = total
        copies.append(pltpu.make_async_copy(held.at[i], out.at[i], sems.at[i]))
        copies[-1].start()
    for copy in copies:
        copy.wait()


def window(directions, adjoint, velocity, diffusivity, objective_source, segment_start):
    dirs, adj, vel, dif, src = (
        directions[0], adjoint[0], velocity[0], diffusivity[0], objective_source[0],
    )
    count, layers, ny, nz = dirs.shape
    fields, part_a = count + 1, (2 * count) // 3
    spaces, segs = lax.axis_size("space"), lax.axis_size("seg")
    assert spaces & (spaces - 1) == 0 and segs & (segs - 1) == 0 and layers >= 3
    odd = lax.axis_index("space") % 2
    place = jnp.stack([odd, lax.axis_index("seg")]).astype(jnp.int32)
    half = jnp.stack([0.5 * modulation(segment_start[0], k) for k in (1, 2)])
    pair_one = [(i, i ^ 1) for i in range(spaces)]
    pair_two = [(i, (i + 1) % spaces if i % 2 else (i - 1) % spaces) for i in range(spaces)]
    f32 = functools.partial(jax.ShapeDtypeStruct, dtype=jnp.float32)
    edge, edge_a, edge_b = (f32((n, ny, nz)) for n in (fields, part_a, fields - part_a))
    layer_bytes = 4 * fields * ny * nz
    layer_flops = 13 * fields * ny * nz
    vs, ss, hs, anys = VMEM_SPEC, SMEM_SPEC, HBM_SPEC, ANY_SPEC
    flow = (vel, dif, src)

    dirs_hbm, adj_hbm = (pltpu.with_memory_space_constraint(x, pltpu.HBM) for x in (dirs, adj))

    def pack(position, start, stop, shape):
        return call(
            functools.partial(pack_kernel, count, layers, position, start, stop), shape,
            [ss, hs, hs], (place, dirs_hbm, adj_hbm),
            scratch=[pltpu.SemaphoreType.DMA((2,))], moved=2 * layer_bytes, grant=2,
        )

    near_a, near_b = call(
        functools.partial(pack_both, count, layers, layers - 1, part_a), [edge_a, edge_b],
        [ss, hs, hs], (place, dirs_hbm, adj_hbm),
        scratch=[pltpu.SemaphoreType.DMA((3,))], moved=2 * layer_bytes, grant=3,
    )
    halo_a = lax.ppermute(near_a, "space", pair_one)
    halo_b = lax.ppermute(near_b, "space", pair_one)
    far = pack(0, 0, fields, edge)
    halo_far = lax.ppermute(far, "space", pair_two)
    inner = call(
        functools.partial(inner_kernel, count, layers), f32((layers - 2, fields, ny, nz)),
        [ss, ss] + [vs] * 5, (place, half, dirs, adj) + flow,
        flops=(layers - 2) * layer_flops, moved=6 * layer_bytes,
    )
    bottom = call(
        functools.partial(bottom_kernel, count, layers), edge,
        [ss, ss] + [vs] * 6, (place, half, dirs, adj, halo_far) + flow,
        flops=layer_flops, moved=4 * layer_bytes,
    )
    bottom_far = lax.ppermute(bottom, "space", pair_two)
    top_a = call(
        functools.partial(top_kernel, count, layers, 0, 0), edge_a,
        [ss, ss] + [vs] * 6 + [anys], (place, half, dirs, adj, halo_a) + flow + (bottom,),
        scratch=[pltpu.SMEM((1,), jnp.int32)],
        flops=layer_flops // 2, moved=2 * layer_bytes,
    )
    near_top_a = lax.ppermute(top_a, "space", pair_one)
    top_b = call(
        functools.partial(top_kernel, count, layers, part_a, TURNS), edge_b,
        [ss, ss] + [vs] * 6 + [anys], (place, half, dirs, adj, halo_b) + flow + (top_a,),
        scratch=[pltpu.SMEM((1,), jnp.int32)],
        flops=layer_flops // 2, moved=2 * layer_bytes,
    )
    near_top_b = lax.ppermute(top_b, "space", pair_one)
    mid, products, early = call(
        functools.partial(middle_kernel, count, layers),
        [f32((layers - 2, fields, ny, nz)), f32((count * SUB, fields * SUB)), f32((layers, ny, nz))],
        [ss, ss] + [vs] * 7, (place, half, bottom, inner, top_a, top_b) + flow,
        flops=4 * (layers - 2) * layer_flops, moved=6 * layer_bytes,
    )
    low, products = call(
        functools.partial(low_kernel, count, layers), [edge, f32((count * SUB, fields * SUB))],
        [ss, ss] + [vs] * 7, (place, half, bottom, inner, bottom_far) + flow + (products,),
        flops=4 * layer_flops, moved=4 * layer_bytes,
    )
    high_a = call(
        functools.partial(high_a_kernel, count, layers), edge_a,
        [ss, ss] + [vs] * 6 + [anys], (place, half, top_a, inner, near_top_a) + flow + (low,),
        flops=layer_flops // 2, moved=2 * layer_bytes,
    )
    high_b, gram = call(
        functools.partial(high_b_kernel, count, layers), [edge_b, f32((count, 128))],
        [ss, ss] + [vs] * 8, (place, half, top_b, inner, near_top_b) + flow + (products, high_a),
        flops=2 * layer_flops, moved=2 * layer_bytes,
    )
    reach = 1
    while reach < spaces:
        gram = gram + lax.ppermute(gram, "space", [(i, i ^ reach) for i in range(spaces)])
        reach *= 2
    piece = f32((layers, ny // segs, nz))
    solved, shadow, *parts = call(
        functools.partial(solve_kernel, count, layers, segs, float(layers * ny * nz * spaces)),
        [f32((count, 128)), f32((layers, ny, nz))] + [piece] * segs,
        [ss] + [vs] * 6, (place, gram, low, mid, high_a, high_b, early),
        flops=4 * layer_flops, moved=4 * layer_bytes,
    )
    gradient = parts[0]
    for k in range(1, segs):
        gradient = gradient + lax.ppermute(parts[k], "seg", [(i, i ^ k) for i in range(segs)])
    basis, factor, along, shadow_out = call(
        functools.partial(basis_kernel, count, layers),
        [f32((count, layers, ny, nz)), f32((count, count)), f32((1, count)), f32((layers, ny, nz))],
        [ss, ss] + [vs] * 6, (place, solved, solved, shadow, low, mid, high_a, high_b),
        scratch=[pltpu.VMEM((count, layers, ny, nz), jnp.float32), pltpu.SemaphoreType.DMA((count + 1,))],
        flops=8 * layer_flops, moved=8 * layer_bytes, out_specs=[hs, vs, vs, hs],
    )
    return basis[None], factor[None], along, shadow_out[None], gradient


def solution(mesh):
    return jax.shard_map(
        window,
        mesh=mesh,
        in_specs=(
            P("seg", None, "space", None, None),
            P("seg", "space", None, None),
            P("seg", None, "space", None, None),
            P("seg", "space", None, None),
            P("seg", "space", None, None),
            P("seg"),
        ),
        out_specs=(
            P("seg", None, "space", None, None),
            P("seg", None, None),
            P("seg", None),
            P("seg", "space", None, None),
            P("space", "seg", None),
        ),
        check_vma=False,
    )
```

```python
import functools
import math

import jax
import jax.numpy as jnp
from jax import lax
from jax.experimental import pallas as pl
from jax.experimental.pallas import tpu as pltpu
from jax.sharding import PartitionSpec as P


SUB = 8
TURNS = 950
HIGH = lax.Precision.HIGHEST
VMEM_SPEC = pl.BlockSpec(memory_space=pltpu.VMEM)
SMEM_SPEC = pl.BlockSpec(memory_space=pltpu.SMEM)
ANY_SPEC = pl.BlockSpec(memory_space=pl.ANY)
HBM_SPEC = pl.BlockSpec(memory_space=pltpu.HBM)


def modulation(window_start, section, shape):
    phase_step = jnp.full(shape, (window_start + 2 - section) & 63, jnp.int32)
    return 1.0 + 0.5 * jnp.sin(2.0 * math.pi * phase_step.astype(jnp.float32) / 64.0)


def call(body, outs, specs, args, scratch=(), flops=0, moved=0, out_specs=None, grant=16):
    return pl.pallas_call(
        body,
        out_shape=outs,
        in_specs=specs,
        out_specs=out_specs or jax.tree.map(lambda _: VMEM_SPEC, outs),
        scratch_shapes=scratch,
        cost_estimate=pl.CostEstimate(flops=flops, transcendentals=0, bytes_accessed=moved),
        compiler_params=pltpu.CompilerParams(vmem_limit_bytes=grant * 1024 * 1024),
    )(*args)


def layer_of(odd, position, layers):
    return position + odd * (layers - 1 - 2 * position)


def pack_kernel(count, layers, position, start, stop, place, dirs, adj, out, sems):
    layer = layer_of(place[0], position, layers)
    size = min(stop, count) - start
    copies = [
        pltpu.make_async_copy(dirs.at[pl.ds(start, size), layer], out.at[pl.ds(0, size)], sems.at[0])
    ]
    if stop > count:
        copies.append(pltpu.make_async_copy(adj.at[layer], out.at[size], sems.at[1]))
    for copy in copies:
        copy.start()
    for copy in copies:
        copy.wait()


def pack_both(count, layers, position, cut, place, dirs, adj, first, second, sems):
    layer = layer_of(place[0], position, layers)
    copies = [
        pltpu.make_async_copy(dirs.at[pl.ds(0, cut), layer], first, sems.at[0]),
        pltpu.make_async_copy(
            dirs.at[pl.ds(cut, count - cut), layer], second.at[pl.ds(0, count - cut)], sems.at[1]
        ),
        pltpu.make_async_copy(adj.at[layer], second.at[count - cut], sems.at[2]),
    ]
    for copy in copies:
        copy.start()
    for copy in copies:
        copy.wait()


def coefficients_at(vel, dif, layer, half, sign, rows, first_row, last_row):
    spread = dif[layer, rows, :]
    ax = (half * sign) * vel[0, layer, rows, :]
    ay = half * vel[1, layer, rows, :]
    az = half * vel[2, layer, rows, :]
    up, down = spread + ay, spread - ay
    row = lax.broadcasted_iota(jnp.int32, spread.shape, 0)
    if last_row:
        up = jnp.where(row == spread.shape[0] - 1, 0.0, up)
    if first_row:
        down = jnp.where(row == 0, 0.0, down)
    return 1.0 - 6.0 * spread, spread + ax, spread - ax, up, down, spread + az, spread - az


def stencil(
    vel, dif, src, layer, half, sign, fields, count, rows_total, width, middle, toward, away, store
):
    for base in range(0, rows_total, SUB):
        rows = slice(base, base + SUB)
        first_row, last_row = base == 0, base + SUB == rows_total
        c0, cxp, cxm, cyp, cym, czp, czm = coefficients_at(
            vel, dif, layer, half, sign, rows, first_row, last_row
        )
        for field in fields:
            tile = middle(field, rows)
            if last_row:
                above = pltpu.roll(tile, SUB - 1, 0)
            else:
                above = middle(field, slice(base + 1, base + 1 + SUB))
            if first_row:
                below = pltpu.roll(tile, 1, 0)
            else:
                below = middle(field, slice(base - 1, base - 1 + SUB))
            total = c0 * tile + cxp * toward(field, rows) + cxm * away(field, rows)
            total = total + (cyp * above + cym * below)
            total = total + (czp * pltpu.roll(tile, width - 1, 1) + czm * pltpu.roll(tile, 1, 1))
            if field == count:
                total = total + src[layer, rows, :]
            store(field, rows, total)


def reader(dirs, adj, count, layer):
    def read(field, rows):
        return dirs[field, layer, rows, :] if field < count else adj[layer, rows, :]

    return read


def plain(ref, *lead):
    def read(field, rows):
        return ref[(*lead, field, rows, slice(None))]

    return read


def joined(first, second):
    cut = first.shape[0]

    def read(field, rows):
        return first[field, rows, :] if field < cut else second[field - cut, rows, :]

    return read


def writer(ref, *lead, start=0):
    def write(field, rows, value):
        ref[(*lead, field - start, rows, slice(None))] = value

    return write


def sign_of(place):
    return (1 - 2 * place[0]).astype(jnp.float32)


def inner_kernel(count, layers, place, window_start, dirs, adj, vel, dif, src, inner, half):
    odd = place[0]
    _, _, ny, nz = dirs.shape
    for k in range(2):
        half[k] = 0.5 * modulation(window_start[0], k + 1, half.shape[1:])
    for position in range(1, layers - 1):
        near, here, far = (layer_of(odd, position + k, layers) for k in (1, 0, -1))
        stencil(
            vel, dif, src, here, half[0], sign_of(place), range(count + 1), count, ny, nz,
            reader(dirs, adj, count, here), reader(dirs, adj, count, near), reader(dirs, adj, count, far),
            writer(inner, position - 1),
        )


def bottom_kernel(count, layers, place, half, dirs, adj, halo, vel, dif, src, edge):
    odd = place[0]
    _, _, ny, nz = dirs.shape
    here, near = layer_of(odd, 0, layers), layer_of(odd, 1, layers)
    stencil(
        vel, dif, src, here, half[0], sign_of(place), range(count + 1), count, ny, nz,
        reader(dirs, adj, count, here), reader(dirs, adj, count, near), plain(halo), writer(edge),
    )


def top_kernel(
    count, layers, start, turns, place, half, dirs, adj, halo, vel, dif, src, order, edge, turned
):
    def turn(step, total):
        turned[0] = turned[0] + step
        return total

    turned[0] = 0
    lax.fori_loop(0, turns * (place[1] % 2), turn, 0)
    odd = place[0]
    _, _, ny, nz = dirs.shape
    here, far = layer_of(odd, layers - 1, layers), layer_of(odd, layers - 2, layers)

    def toward(field, rows):
        return halo[field - start, rows, :]

    stencil(
        vel, dif, src, here, half[0], sign_of(place), range(start, start + edge.shape[0]), count, ny, nz,
        reader(dirs, adj, count, here), toward, reader(dirs, adj, count, far), writer(edge, start=start),
    )


def add_products(tiles, count, ny, total):
    step = 2 * SUB if ny % (2 * SUB) == 0 else SUB
    for base in range(0, ny, step):
        parts = [tiles(slice(row, row + SUB)) for row in range(base, base + step, SUB)]
        block = jnp.concatenate(parts, axis=1) if len(parts) > 1 else parts[0]
        total = total + lax.dot_general(
            block[: count * SUB], block, (((1,), (1,)), ((), ())),
            precision=HIGH, preferred_element_type=jnp.float32,
        )
    return total


def flat(tile):
    return tile.reshape(tile.shape[0] * tile.shape[1], tile.shape[2])


def middle_kernel(
    count, layers, place, half, bottom, inner, top_a, top_b, vel, dif, src, out, products, early
):
    odd = place[0]
    _, ny, nz = bottom.shape

    def at(position):
        if position == 0:
            return plain(bottom)
        return joined(top_a, top_b) if position == layers - 1 else plain(inner, position - 1)

    for position in range(1, layers - 1):
        stencil(
            vel, dif, src, layer_of(odd, position, layers), half[1], sign_of(place), range(count + 1),
            count, ny, nz, at(position), at(position + 1), at(position - 1), writer(out, position - 1),
        )
    for position in range(layers):
        early[layer_of(odd, position, layers)] = at(position)(count, slice(0, ny))
    total = jnp.zeros(products.shape, jnp.float32)
    for position in range(1, layers - 1):
        total = add_products(lambda rows: flat(out[position - 1, :, rows, :]), count, ny, total)
    products[...] = total


def low_kernel(count, layers, place, half, bottom, inner, halo, vel, dif, src, before, out, products):
    odd = place[0]
    _, ny, nz = bottom.shape
    stencil(
        vel, dif, src, layer_of(odd, 0, layers), half[1], sign_of(place), range(count + 1), count, ny, nz,
        plain(bottom), plain(inner, 0), plain(halo), writer(out),
    )
    products[...] = add_products(lambda rows: flat(out[:, rows, :]), count, ny, before[...])


def high_stencil(count, layers, start, place, half, top, inner, halo, vel, dif, src, out):
    _, ny, nz = top.shape

    def middle(field, rows):
        return top[field - start, rows, :]

    def toward(field, rows):
        return halo[field - start, rows, :]

    stencil(
        vel, dif, src, layer_of(place[0], layers - 1, layers), half[1], sign_of(place),
        range(start, start + out.shape[0]), count, ny, nz, middle, toward, plain(inner, layers - 3),
        writer(out, start=start),
    )


def high_a_kernel(count, layers, place, half, top, inner, halo, vel, dif, src, order, out):
    high_stencil(count, layers, 0, place, half, top, inner, halo, vel, dif, src, out)


def high_b_kernel(
    count, layers, place, half, top, inner, halo, vel, dif, src, before, out_a, out, gram
):
    start = out_a.shape[0]
    _, ny, _ = top.shape
    high_stencil(count, layers, start, place, half, top, inner, halo, vel, dif, src, out)
    total = add_products(
        lambda rows: jnp.concatenate([flat(out_a[:, rows, :]), flat(out[:, rows, :])], axis=0),
        count, ny, before[...],
    )
    rows = lax.broadcasted_iota(jnp.int32, total.shape, 0)
    columns = lax.broadcasted_iota(jnp.int32, total.shape, 1)
    total = jnp.where(rows % SUB == columns % SUB, total, 0.0)
    total = total.reshape(count, SUB, total.shape[1]).sum(axis=1)
    width = gram.shape[1]
    gather = (
        lax.broadcasted_iota(jnp.int32, (total.shape[1], width), 0) // SUB
        == lax.broadcasted_iota(jnp.int32, (total.shape[1], width), 1)
    ).astype(jnp.float32)
    gram[...] = jnp.dot(total, gather, precision=HIGH, preferred_element_type=jnp.float32)


def result_at(position, layers, low, mid, high_a, high_b):
    if position == 0:
        return plain(low)
    return joined(high_a, high_b) if position == layers - 1 else plain(mid, position - 1)


def solve_kernel(
    count, layers, pieces, cells, place, gram, low, mid, high_a, high_b, early, solved, shadow, *parts
):
    odd, seg = place[0], place[1]
    _, ny, nz = low.shape
    shape = gram.shape
    row = lax.broadcasted_iota(jnp.int32, shape, 0)
    lane = lax.broadcasted_iota(jnp.int32, shape, 1)
    table = jnp.where(lane <= count, gram[...] / cells, 0.0)
    table = jnp.where(lane == row + count + 1, 1.0, table)
    scale = jnp.ones(shape, jnp.float32)
    columns = [jnp.broadcast_to(table[:, j : j + 1], shape) for j in range(count)]
    for k in range(count):
        pivot = jnp.broadcast_to(columns[k][k : k + 1, :], shape)
        scale = jnp.where(row == k, pivot, scale)
        ratio = jnp.where(row > k, columns[k] * (1.0 / pivot), 0.0)
        for j in range(k + 1, count):
            columns[j] = columns[j] - ratio * jnp.broadcast_to(columns[j][k : k + 1, :], shape)
        table = table - ratio * jnp.broadcast_to(table[k : k + 1, :], shape)
    table = table / jnp.sqrt(scale)
    table = jnp.where((lane < count) & (lane < row), 0.0, table)
    solved[...] = table
    weights = jnp.sum(table[:, count : count + 1] * table, axis=0, keepdims=True)
    splat = [
        jnp.broadcast_to(weights[:, count + 1 + j : count + 2 + j], (SUB, nz)) for j in range(count)
    ]
    for position in range(layers):
        layer = layer_of(odd, position, layers)
        read = result_at(position, layers, low, mid, high_a, high_b)
        for base in range(0, ny, SUB):
            rows = slice(base, base + SUB)
            total = read(count, rows)
            for j in range(count):
                total = total - splat[j] * read(j, rows)
            shadow[layer, rows, :] = total
    step = ny // pieces
    for k, part in enumerate(parts):
        begin = pl.multiple_of((seg ^ k) * step, step)
        rows = pl.ds(begin, step)
        part[...] = shadow[:, rows, :] + early[:, rows, :]


def basis_kernel(
    count, layers, place, weights, solved, shadow, low, mid, high_a, high_b,
    out, factor, along, shadow_out, held, sems,
):
    odd = place[0]
    _, ny, _ = low.shape
    block = min(ny, 8 * SUB)
    copies = [pltpu.make_async_copy(shadow, shadow_out, sems.at[count])]
    copies[0].start()
    table = solved[...]
    factor[...] = table[:, :count]
    eye = (
        lax.broadcasted_iota(jnp.int32, (count, count), 0) == lax.broadcasted_iota(jnp.int32, (count, count), 1)
    )
    along[...] = jnp.sum(jnp.where(eye, table[:, count : count + 1], 0.0), axis=0, keepdims=True)
    for i in range(count):
        for position in range(layers):
            layer = layer_of(odd, position, layers)
            read = result_at(position, layers, low, mid, high_a, high_b)
            for base in range(0, ny, block):
                rows = slice(base, base + block)
                total = weights[i, count + 1] * read(0, rows)
                for j in range(1, i + 1):
                    total = total + weights[i, count + 1 + j] * read(j, rows)
                held[i, layer, rows, :] = total
        copies.append(pltpu.make_async_copy(held.at[i], out.at[i], sems.at[i]))
        copies[-1].start()
    for copy in copies:
        copy.wait()


def window(directions, adjoint, velocity, diffusivity, objective_source, segment_start):
    dirs, adj, vel, dif, src = (
        directions[0], adjoint[0], velocity[0], diffusivity[0], objective_source[0],
    )
    count, layers, ny, nz = dirs.shape
    fields, part_a = count + 1, (2 * count) // 3
    spaces, segs = lax.axis_size("space"), lax.axis_size("seg")
    assert spaces & (spaces - 1) == 0 and segs & (segs - 1) == 0 and layers >= 3
    odd = lax.axis_index("space") % 2
    place = jnp.stack([odd, lax.axis_index("seg")]).astype(jnp.int32)
    pair_one = [(i, i ^ 1) for i in range(spaces)]
    pair_two = [(i, (i + 1) % spaces if i % 2 else (i - 1) % spaces) for i in range(spaces)]
    f32 = functools.partial(jax.ShapeDtypeStruct, dtype=jnp.float32)
    edge, edge_a, edge_b = (f32((n, ny, nz)) for n in (fields, part_a, fields - part_a))
    layer_bytes = 4 * fields * ny * nz
    layer_flops = 13 * fields * ny * nz
    vs, ss, hs, anys = VMEM_SPEC, SMEM_SPEC, HBM_SPEC, ANY_SPEC
    flow = (vel, dif, src)

    dirs_hbm, adj_hbm = (pltpu.with_memory_space_constraint(x, pltpu.HBM) for x in (dirs, adj))

    def pack(position, start, stop, shape):
        return call(
            functools.partial(pack_kernel, count, layers, position, start, stop), shape,
            [ss, hs, hs], (place, dirs_hbm, adj_hbm),
            scratch=[pltpu.SemaphoreType.DMA((2,))], moved=2 * layer_bytes, grant=2,
        )

    near_a, near_b = call(
        functools.partial(pack_both, count, layers, layers - 1, part_a), [edge_a, edge_b],
        [ss, hs, hs], (place, dirs_hbm, adj_hbm),
        scratch=[pltpu.SemaphoreType.DMA((3,))], moved=2 * layer_bytes, grant=3,
    )
    halo_a = lax.ppermute(near_a, "space", pair_one)
    halo_b = lax.ppermute(near_b, "space", pair_one)
    far = pack(0, 0, fields, edge)
    halo_far = lax.ppermute(far, "space", pair_two)
    inner, half = call(
        functools.partial(inner_kernel, count, layers),
        [f32((layers - 2, fields, ny, nz)), f32((2, SUB, nz))],
        [ss, ss] + [vs] * 5, (place, segment_start, dirs, adj) + flow,
        flops=(layers - 2) * layer_flops, moved=6 * layer_bytes,
    )
    bottom = call(
        functools.partial(bottom_kernel, count, layers), edge,
        [ss] + [vs] * 7, (place, half, dirs, adj, halo_far) + flow,
        flops=layer_flops, moved=4 * layer_bytes,
    )
    bottom_far = lax.ppermute(bottom, "space", pair_two)
    top_a = call(
        functools.partial(top_kernel, count, layers, 0, 0), edge_a,
        [ss] + [vs] * 7 + [anys], (place, half, dirs, adj, halo_a) + flow + (bottom,),
        scratch=[pltpu.SMEM((1,), jnp.int32)],
        flops=layer_flops // 2, moved=2 * layer_bytes,
    )
    near_top_a = lax.ppermute(top_a, "space", pair_one)
    top_b = call(
        functools.partial(top_kernel, count, layers, part_a, TURNS), edge_b,
        [ss] + [vs] * 7 + [anys], (place, half, dirs, adj, halo_b) + flow + (top_a,),
        scratch=[pltpu.SMEM((1,), jnp.int32)],
        flops=layer_flops // 2, moved=2 * layer_bytes,
    )
    near_top_b = lax.ppermute(top_b, "space", pair_one)
    mid, products, early = call(
        functools.partial(middle_kernel, count, layers),
        [f32((layers - 2, fields, ny, nz)), f32((count * SUB, fields * SUB)), f32((layers, ny, nz))],
        [ss] + [vs] * 8, (place, half, bottom, inner, top_a, top_b) + flow,
        flops=4 * (layers - 2) * layer_flops, moved=6 * layer_bytes,
    )
    low, products = call(
        functools.partial(low_kernel, count, layers), [edge, f32((count * SUB, fields * SUB))],
        [ss] + [vs] * 8, (place, half, bottom, inner, bottom_far) + flow + (products,),
        flops=4 * layer_flops, moved=4 * layer_bytes,
    )
    high_a = call(
        functools.partial(high_a_kernel, count, layers), edge_a,
        [ss] + [vs] * 7 + [anys], (place, half, top_a, inner, near_top_a) + flow + (low,),
        flops=layer_flops // 2, moved=2 * layer_bytes,
    )
    high_b, gram = call(
        functools.partial(high_b_kernel, count, layers), [edge_b, f32((count, 128))],
        [ss] + [vs] * 9, (place, half, top_b, inner, near_top_b) + flow + (products, high_a),
        flops=2 * layer_flops, moved=2 * layer_bytes,
    )
    reach = 1
    while reach < spaces:
        gram = gram + lax.ppermute(gram, "space", [(i, i ^ reach) for i in range(spaces)])
        reach *= 2
    piece = f32((layers, ny // segs, nz))
    solved, shadow, *parts = call(
        functools.partial(solve_kernel, count, layers, segs, float(layers * ny * nz * spaces)),
        [f32((count, 128)), f32((layers, ny, nz))] + [piece] * segs,
        [ss] + [vs] * 6, (place, gram, low, mid, high_a, high_b, early),
        flops=4 * layer_flops, moved=4 * layer_bytes,
    )
    gradient = parts[0]
    for k in range(1, segs):
        gradient = gradient + lax.ppermute(parts[k], "seg", [(i, i ^ k) for i in range(segs)])
    basis, factor, along, shadow_out = call(
        functools.partial(basis_kernel, count, layers),
        [f32((count, layers, ny, nz)), f32((count, count)), f32((1, count)), f32((layers, ny, nz))],
        [ss, ss] + [vs] * 6, (place, solved, solved, shadow, low, mid, high_a, high_b),
        scratch=[pltpu.VMEM((count, layers, ny, nz), jnp.float32), pltpu.SemaphoreType.DMA((count + 1,))],
        flops=8 * layer_flops, moved=8 * layer_bytes, out_specs=[hs, vs, vs, hs],
    )
    return basis[None], factor[None], along, shadow_out[None], gradient


def solution(mesh):
    return jax.shard_map(
        window,
        mesh=mesh,
        in_specs=(
            P("seg", None, "space", None, None),
            P("seg", "space", None, None),
            P("seg", None, "space", None, None),
            P("seg", "space", None, None),
            P("seg", "space", None, None),
            P("seg"),
        ),
        out_specs=(
            P("seg", None, "space", None, None),
            P("seg", None, None),
            P("seg", None),
            P("seg", "space", None, None),
            P("space", "seg", None),
        ),
        check_vma=False,
    )
```

```python
import functools
import math

import jax
import jax.numpy as jnp
from jax import lax
from jax.experimental import pallas as pl
from jax.experimental.pallas import tpu as pltpu
from jax.sharding import PartitionSpec as P


SUB = 8
TURNS = 900
HIGH = lax.Precision.HIGHEST
VMEM_SPEC = pl.BlockSpec(memory_space=pltpu.VMEM)
SMEM_SPEC = pl.BlockSpec(memory_space=pltpu.SMEM)
ANY_SPEC = pl.BlockSpec(memory_space=pl.ANY)
HBM_SPEC = pl.BlockSpec(memory_space=pltpu.HBM)


def modulation(window_start, section, shape):
    phase_step = jnp.full(shape, (window_start + 2 - section) & 63, jnp.int32)
    return 1.0 + 0.5 * jnp.sin(2.0 * math.pi * phase_step.astype(jnp.float32) / 64.0)


def call(body, outs, specs, args, scratch=(), flops=0, moved=0, out_specs=None, grant=16):
    return pl.pallas_call(
        body,
        out_shape=outs,
        in_specs=specs,
        out_specs=out_specs or jax.tree.map(lambda _: VMEM_SPEC, outs),
        scratch_shapes=scratch,
        cost_estimate=pl.CostEstimate(flops=flops, transcendentals=0, bytes_accessed=moved),
        compiler_params=pltpu.CompilerParams(vmem_limit_bytes=grant * 1024 * 1024),
    )(*args)


def layer_of(odd, position, layers):
    return position + odd * (layers - 1 - 2 * position)


def pack_kernel(count, layers, position, start, stop, place, dirs, adj, out, sems):
    layer = layer_of(place[0], position, layers)
    size = min(stop, count) - start
    copies = [
        pltpu.make_async_copy(dirs.at[pl.ds(start, size), layer], out.at[pl.ds(0, size)], sems.at[0])
    ]
    if stop > count:
        copies.append(pltpu.make_async_copy(adj.at[layer], out.at[size], sems.at[1]))
    for copy in copies:
        copy.start()
    for copy in copies:
        copy.wait()


def pack_both(count, layers, position, cut, place, dirs, adj, first, second, sems):
    layer = layer_of(place[0], position, layers)
    copies = [
        pltpu.make_async_copy(dirs.at[pl.ds(0, cut), layer], first, sems.at[0]),
        pltpu.make_async_copy(
            dirs.at[pl.ds(cut, count - cut), layer], second.at[pl.ds(0, count - cut)], sems.at[1]
        ),
        pltpu.make_async_copy(adj.at[layer], second.at[count - cut], sems.at[2]),
    ]
    for copy in copies:
        copy.start()
    for copy in copies:
        copy.wait()


def coefficients_at(vel, dif, layer, half, sign, rows, first_row, last_row):
    spread = dif[layer, rows, :]
    ax = (half * sign) * vel[0, layer, rows, :]
    ay = half * vel[1, layer, rows, :]
    az = half * vel[2, layer, rows, :]
    up, down = spread + ay, spread - ay
    row = lax.broadcasted_iota(jnp.int32, spread.shape, 0)
    if last_row:
        up = jnp.where(row == spread.shape[0] - 1, 0.0, up)
    if first_row:
        down = jnp.where(row == 0, 0.0, down)
    return 1.0 - 6.0 * spread, spread + ax, spread - ax, up, down, spread + az, spread - az


def stencil(
    vel, dif, src, layer, half, sign, fields, count, rows_total, width, middle, toward, away, store
):
    for base in range(0, rows_total, SUB):
        rows = slice(base, base + SUB)
        first_row, last_row = base == 0, base + SUB == rows_total
        c0, cxp, cxm, cyp, cym, czp, czm = coefficients_at(
            vel, dif, layer, half, sign, rows, first_row, last_row
        )
        for field in fields:
            tile = middle(field, rows)
            if last_row:
                above = pltpu.roll(tile, SUB - 1, 0)
            else:
                above = middle(field, slice(base + 1, base + 1 + SUB))
            if first_row:
                below = pltpu.roll(tile, 1, 0)
            else:
                below = middle(field, slice(base - 1, base - 1 + SUB))
            total = c0 * tile + cxp * toward(field, rows) + cxm * away(field, rows)
            total = total + (cyp * above + cym * below)
            total = total + (czp * pltpu.roll(tile, width - 1, 1) + czm * pltpu.roll(tile, 1, 1))
            if field == count:
                total = total + src[layer, rows, :]
            store(field, rows, total)


def reader(dirs, adj, count, layer):
    def read(field, rows):
        return dirs[field, layer, rows, :] if field < count else adj[layer, rows, :]

    return read


def plain(ref, *lead):
    def read(field, rows):
        return ref[(*lead, field, rows, slice(None))]

    return read


def joined(first, second):
    cut = first.shape[0]

    def read(field, rows):
        return first[field, rows, :] if field < cut else second[field - cut, rows, :]

    return read


def writer(ref, *lead, start=0):
    def write(field, rows, value):
        ref[(*lead, field - start, rows, slice(None))] = value

    return write


def sign_of(place):
    return (1 - 2 * place[0]).astype(jnp.float32)


def inner_kernel(count, layers, place, window_start, dirs_far, adj, vel, dif, src, inner, half, dirs, sem):
    odd = place[0]
    fetch = pltpu.make_async_copy(dirs_far, dirs, sem)
    fetch.start()
    fetch.wait()
    _, _, ny, nz = dirs.shape
    for k in range(2):
        half[k] = 0.5 * modulation(window_start[0], k + 1, half.shape[1:])
    for position in range(1, layers - 1):
        near, here, far = (layer_of(odd, position + k, layers) for k in (1, 0, -1))
        stencil(
            vel, dif, src, here, half[0], sign_of(place), range(count + 1), count, ny, nz,
            reader(dirs, adj, count, here), reader(dirs, adj, count, near), reader(dirs, adj, count, far),
            writer(inner, position - 1),
        )


def bottom_kernel(count, layers, place, half, dirs, adj, halo, vel, dif, src, edge):
    odd = place[0]
    _, _, ny, nz = dirs.shape
    here, near = layer_of(odd, 0, layers), layer_of(odd, 1, layers)
    stencil(
        vel, dif, src, here, half[0], sign_of(place), range(count + 1), count, ny, nz,
        reader(dirs, adj, count, here), reader(dirs, adj, count, near), plain(halo), writer(edge),
    )


def top_kernel(
    count, layers, start, turns, place, half, dirs, adj, halo, vel, dif, src, order, edge, turned
):
    def turn(step, total):
        turned[0] = turned[0] + step
        return total

    turned[0] = 0
    lax.fori_loop(0, turns * (place[1] % 2), turn, 0)
    odd = place[0]
    _, _, ny, nz = dirs.shape
    here, far = layer_of(odd, layers - 1, layers), layer_of(odd, layers - 2, layers)

    def toward(field, rows):
        return halo[field - start, rows, :]

    stencil(
        vel, dif, src, here, half[0], sign_of(place), range(start, start + edge.shape[0]), count, ny, nz,
        reader(dirs, adj, count, here), toward, reader(dirs, adj, count, far), writer(edge, start=start),
    )


def add_products(tiles, count, ny, total):
    step = 2 * SUB if ny % (2 * SUB) == 0 else SUB
    for base in range(0, ny, step):
        parts = [tiles(slice(row, row + SUB)) for row in range(base, base + step, SUB)]
        block = jnp.concatenate(parts, axis=1) if len(parts) > 1 else parts[0]
        total = total + lax.dot_general(
            block[: count * SUB], block, (((1,), (1,)), ((), ())),
            precision=HIGH, preferred_element_type=jnp.float32,
        )
    return total


def flat(tile):
    return tile.reshape(tile.shape[0] * tile.shape[1], tile.shape[2])


def middle_kernel(
    count, layers, place, half, bottom, inner, top_a, top_b, vel, dif, src, out, products, early
):
    odd = place[0]
    _, ny, nz = bottom.shape

    def at(position):
        if position == 0:
            return plain(bottom)
        return joined(top_a, top_b) if position == layers - 1 else plain(inner, position - 1)

    for position in range(1, layers - 1):
        stencil(
            vel, dif, src, layer_of(odd, position, layers), half[1], sign_of(place), range(count + 1),
            count, ny, nz, at(position), at(position + 1), at(position - 1), writer(out, position - 1),
        )
    for position in range(layers):
        early[layer_of(odd, position, layers)] = at(position)(count, slice(0, ny))
    total = jnp.zeros(products.shape, jnp.float32)
    for position in range(1, layers - 1):
        total = add_products(lambda rows: flat(out[position - 1, :, rows, :]), count, ny, total)
    products[...] = total


def low_kernel(count, layers, place, half, bottom, inner, halo, vel, dif, src, before, out, products):
    odd = place[0]
    _, ny, nz = bottom.shape
    stencil(
        vel, dif, src, layer_of(odd, 0, layers), half[1], sign_of(place), range(count + 1), count, ny, nz,
        plain(bottom), plain(inner, 0), plain(halo), writer(out),
    )
    products[...] = add_products(lambda rows: flat(out[:, rows, :]), count, ny, before[...])


def high_stencil(count, layers, start, place, half, top, inner, halo, vel, dif, src, out):
    _, ny, nz = top.shape

    def middle(field, rows):
        return top[field - start, rows, :]

    def toward(field, rows):
        return halo[field - start, rows, :]

    stencil(
        vel, dif, src, layer_of(place[0], layers - 1, layers), half[1], sign_of(place),
        range(start, start + out.shape[0]), count, ny, nz, middle, toward, plain(inner, layers - 3),
        writer(out, start=start),
    )


def high_a_kernel(count, layers, place, half, top, inner, halo, vel, dif, src, order, out):
    high_stencil(count, layers, 0, place, half, top, inner, halo, vel, dif, src, out)


def high_b_kernel(
    count, layers, place, half, top, inner, halo, vel, dif, src, before, out_a, out, gram
):
    start = out_a.shape[0]
    _, ny, _ = top.shape
    high_stencil(count, layers, start, place, half, top, inner, halo, vel, dif, src, out)
    total = add_products(
        lambda rows: jnp.concatenate([flat(out_a[:, rows, :]), flat(out[:, rows, :])], axis=0),
        count, ny, before[...],
    )
    rows = lax.broadcasted_iota(jnp.int32, total.shape, 0)
    columns = lax.broadcasted_iota(jnp.int32, total.shape, 1)
    total = jnp.where(rows % SUB == columns % SUB, total, 0.0)
    total = total.reshape(count, SUB, total.shape[1]).sum(axis=1)
    width = gram.shape[1]
    gather = (
        lax.broadcasted_iota(jnp.int32, (total.shape[1], width), 0) // SUB
        == lax.broadcasted_iota(jnp.int32, (total.shape[1], width), 1)
    ).astype(jnp.float32)
    gram[...] = jnp.dot(total, gather, precision=HIGH, preferred_element_type=jnp.float32)


def result_at(position, layers, low, mid, high_a, high_b):
    if position == 0:
        return plain(low)
    return joined(high_a, high_b) if position == layers - 1 else plain(mid, position - 1)


def solve_kernel(
    count, layers, pieces, cells, place, gram, low, mid, high_a, high_b, early, solved, shadow, *parts
):
    odd, seg = place[0], place[1]
    _, ny, nz = low.shape
    shape = gram.shape
    row = lax.broadcasted_iota(jnp.int32, shape, 0)
    lane = lax.broadcasted_iota(jnp.int32, shape, 1)
    table = jnp.where(lane <= count, gram[...] / cells, 0.0)
    table = jnp.where(lane == row + count + 1, 1.0, table)
    scale = jnp.ones(shape, jnp.float32)
    columns = [jnp.broadcast_to(table[:, j : j + 1], shape) for j in range(count)]
    for k in range(count):
        pivot = jnp.broadcast_to(columns[k][k : k + 1, :], shape)
        scale = jnp.where(row == k, pivot, scale)
        ratio = jnp.where(row > k, columns[k] * (1.0 / pivot), 0.0)
        for j in range(k + 1, count):
            columns[j] = columns[j] - ratio * jnp.broadcast_to(columns[j][k : k + 1, :], shape)
        table = table - ratio * jnp.broadcast_to(table[k : k + 1, :], shape)
    table = table / jnp.sqrt(scale)
    table = jnp.where((lane < count) & (lane < row), 0.0, table)
    solved[...] = table
    weights = jnp.sum(table[:, count : count + 1] * table, axis=0, keepdims=True)
    splat = [
        jnp.broadcast_to(weights[:, count + 1 + j : count + 2 + j], (SUB, nz)) for j in range(count)
    ]
    for position in range(layers):
        layer = layer_of(odd, position, layers)
        read = result_at(position, layers, low, mid, high_a, high_b)
        for base in range(0, ny, SUB):
            rows = slice(base, base + SUB)
            total = read(count, rows)
            for j in range(count):
                total = total - splat[j] * read(j, rows)
            shadow[layer, rows, :] = total
    step = ny // pieces
    for k, part in enumerate(parts):
        begin = pl.multiple_of((seg ^ k) * step, step)
        rows = pl.ds(begin, step)
        part[...] = shadow[:, rows, :] + early[:, rows, :]


def basis_kernel(
    count, layers, place, weights, solved, shadow, low, mid, high_a, high_b,
    out, factor, along, shadow_out, held, sems,
):
    odd = place[0]
    _, ny, _ = low.shape
    block = min(ny, 8 * SUB)
    copies = [pltpu.make_async_copy(shadow, shadow_out, sems.at[count])]
    copies[0].start()
    table = solved[...]
    factor[...] = table[:, :count]
    eye = (
        lax.broadcasted_iota(jnp.int32, (count, count), 0) == lax.broadcasted_iota(jnp.int32, (count, count), 1)
    )
    along[...] = jnp.sum(jnp.where(eye, table[:, count : count + 1], 0.0), axis=0, keepdims=True)
    for i in range(count):
        for position in range(layers):
            layer = layer_of(odd, position, layers)
            read = result_at(position, layers, low, mid, high_a, high_b)
            for base in range(0, ny, block):
                rows = slice(base, base + block)
                total = weights[i, count + 1] * read(0, rows)
                for j in range(1, i + 1):
                    total = total + weights[i, count + 1 + j] * read(j, rows)
                held[i, layer, rows, :] = total
        copies.append(pltpu.make_async_copy(held.at[i], out.at[i], sems.at[i]))
        copies[-1].start()
    for copy in copies:
        copy.wait()


def window(directions, adjoint, velocity, diffusivity, objective_source, segment_start):
    dirs, adj, vel, dif, src = (
        directions[0], adjoint[0], velocity[0], diffusivity[0], objective_source[0],
    )
    count, layers, ny, nz = dirs.shape
    fields, part_a = count + 1, (2 * count) // 3
    spaces, segs = lax.axis_size("space"), lax.axis_size("seg")
    assert spaces & (spaces - 1) == 0 and segs & (segs - 1) == 0 and layers >= 3
    odd = lax.axis_index("space") % 2
    place = jnp.stack([odd, lax.axis_index("seg")]).astype(jnp.int32)
    pair_one = [(i, i ^ 1) for i in range(spaces)]
    pair_two = [(i, (i + 1) % spaces if i % 2 else (i - 1) % spaces) for i in range(spaces)]
    f32 = functools.partial(jax.ShapeDtypeStruct, dtype=jnp.float32)
    edge, edge_a, edge_b = (f32((n, ny, nz)) for n in (fields, part_a, fields - part_a))
    layer_bytes = 4 * fields * ny * nz
    layer_flops = 13 * fields * ny * nz
    vs, ss, hs, anys = VMEM_SPEC, SMEM_SPEC, HBM_SPEC, ANY_SPEC
    flow = (vel, dif, src)

    dirs_hbm, adj_hbm = (pltpu.with_memory_space_constraint(x, pltpu.HBM) for x in (dirs, adj))

    def pack(position, start, stop, shape):
        return call(
            functools.partial(pack_kernel, count, layers, position, start, stop), shape,
            [ss, hs, hs], (place, dirs_hbm, adj_hbm),
            scratch=[pltpu.SemaphoreType.DMA((2,))], moved=2 * layer_bytes, grant=2,
        )

    near_a, near_b = call(
        functools.partial(pack_both, count, layers, layers - 1, part_a), [edge_a, edge_b],
        [ss, hs, hs], (place, dirs_hbm, adj_hbm),
        scratch=[pltpu.SemaphoreType.DMA((3,))], moved=2 * layer_bytes, grant=3,
    )
    halo_a = lax.ppermute(near_a, "space", pair_one)
    halo_b = lax.ppermute(near_b, "space", pair_one)
    far = pack(0, 0, fields, edge)
    halo_far = lax.ppermute(far, "space", pair_two)
    inner, half, dirs = call(
        functools.partial(inner_kernel, count, layers),
        [f32((layers - 2, fields, ny, nz)), f32((2, SUB, nz)), f32((count, layers, ny, nz))],
        [ss, ss, hs] + [vs] * 4, (place, segment_start, dirs_hbm, adj) + flow,
        scratch=[pltpu.SemaphoreType.DMA],
        flops=(layers - 2) * layer_flops, moved=6 * layer_bytes,
    )
    bottom = call(
        functools.partial(bottom_kernel, count, layers), edge,
        [ss] + [vs] * 7, (place, half, dirs, adj, halo_far) + flow,
        flops=layer_flops, moved=4 * layer_bytes,
    )
    bottom_far = lax.ppermute(bottom, "space", pair_two)
    top_a = call(
        functools.partial(top_kernel, count, layers, 0, 0), edge_a,
        [ss] + [vs] * 7 + [anys], (place, half, dirs, adj, halo_a) + flow + (bottom,),
        scratch=[pltpu.SMEM((1,), jnp.int32)],
        flops=layer_flops // 2, moved=2 * layer_bytes,
    )
    near_top_a = lax.ppermute(top_a, "space", pair_one)
    top_b = call(
        functools.partial(top_kernel, count, layers, part_a, TURNS), edge_b,
        [ss] + [vs] * 7 + [anys], (place, half, dirs, adj, halo_b) + flow + (top_a,),
        scratch=[pltpu.SMEM((1,), jnp.int32)],
        flops=layer_flops // 2, moved=2 * layer_bytes,
    )
    near_top_b = lax.ppermute(top_b, "space", pair_one)
    mid, products, early = call(
        functools.partial(middle_kernel, count, layers),
        [f32((layers - 2, fields, ny, nz)), f32((count * SUB, fields * SUB)), f32((layers, ny, nz))],
        [ss] + [vs] * 8, (place, half, bottom, inner, top_a, top_b) + flow,
        flops=4 * (layers - 2) * layer_flops, moved=6 * layer_bytes,
    )
    low, products = call(
        functools.partial(low_kernel, count, layers), [edge, f32((count * SUB, fields * SUB))],
        [ss] + [vs] * 8, (place, half, bottom, inner, bottom_far) + flow + (products,),
        flops=4 * layer_flops, moved=4 * layer_bytes,
    )
    high_a = call(
        functools.partial(high_a_kernel, count, layers), edge_a,
        [ss] + [vs] * 7 + [anys], (place, half, top_a, inner, near_top_a) + flow + (low,),
        flops=layer_flops // 2, moved=2 * layer_bytes,
    )
    high_b, gram = call(
        functools.partial(high_b_kernel, count, layers), [edge_b, f32((count, 128))],
        [ss] + [vs] * 9, (place, half, top_b, inner, near_top_b) + flow + (products, high_a),
        flops=2 * layer_flops, moved=2 * layer_bytes,
    )
    reach = 1
    while reach < spaces:
        gram = gram + lax.ppermute(gram, "space", [(i, i ^ reach) for i in range(spaces)])
        reach *= 2
    piece = f32((layers, ny // segs, nz))
    solved, shadow, *parts = call(
        functools.partial(solve_kernel, count, layers, segs, float(layers * ny * nz * spaces)),
        [f32((count, 128)), f32((layers, ny, nz))] + [piece] * segs,
        [ss] + [vs] * 6, (place, gram, low, mid, high_a, high_b, early),
        flops=4 * layer_flops, moved=4 * layer_bytes,
    )
    gradient = parts[0]
    for k in range(1, segs):
        gradient = gradient + lax.ppermute(parts[k], "seg", [(i, i ^ k) for i in range(segs)])
    basis, factor, along, shadow_out = call(
        functools.partial(basis_kernel, count, layers),
        [f32((count, layers, ny, nz)), f32((count, count)), f32((1, count)), f32((layers, ny, nz))],
        [ss, ss] + [vs] * 6, (place, solved, solved, shadow, low, mid, high_a, high_b),
        scratch=[pltpu.VMEM((count, layers, ny, nz), jnp.float32), pltpu.SemaphoreType.DMA((count + 1,))],
        flops=8 * layer_flops, moved=8 * layer_bytes, out_specs=[hs, vs, vs, hs],
    )
    return basis[None], factor[None], along, shadow_out[None], gradient


def solution(mesh):
    return jax.shard_map(
        window,
        mesh=mesh,
        in_specs=(
            P("seg", None, "space", None, None),
            P("seg", "space", None, None),
            P("seg", None, "space", None, None),
            P("seg", "space", None, None),
            P("seg", "space", None, None),
            P("seg"),
        ),
        out_specs=(
            P("seg", None, "space", None, None),
            P("seg", None, None),
            P("seg", None),
            P("seg", "space", None, None),
            P("space", "seg", None),
        ),
        check_vma=False,
    )
```
